32 devices in a mesh: ctx: 8 (over y, x, core), head: 4 (over z).
Axes of the slice: x: 2, y: 2, z: 4, core: 2. Of those that a mesh axis runs over, the one named last changes fastest.
Arguments:
- query_key: bfloat16 [4096, 1024], P('ctx', 'head'), may hold values from -6 to 6
- values: bfloat16 [4096, 4096], P('ctx', 'head'), may hold values from -6 to 6
- out_grad: bfloat16 [4096, 4096], P('ctx', 'head'), may hold values from -6 to 6
- out_weight: bfloat16 [4096, 4096], P('head'), may hold values from -0.09375 to 0.09375
- doc_lengths: int32 [32], replicated, may hold values from 1 to 2048, 4096 in all
Outputs:
- qk_grad: bfloat16 [4096, 1024], P('ctx', 'head')
- value_grad: bfloat16 [4096, 4096], P('ctx', 'head')
- proj_grad: float32 [4096, 4096], P('head', 'ctx')
The draws below stay inside these ranges and needn't reach their ends.
Inputs may be any that keep to these rules, and one draw needn't show every extreme that they name: `doc_lengths`: the documents fill all 4096 positions in order; the longest has exactly 2048 tokens.
All inputs are finite; a program needn't handle non-finite values.
Results may differ from the reference program's by a relative error of at most 0.0068.
Values may be sent and summed in bfloat16 or wider, within the bound.
A program may use at most 128 MiB of HBM per device.

```python
import math
import jax
import jax.numpy as jnp
import numpy as np
from jax import lax

D = 4096
H = 32
HEAD = 128
QK = 16
FEAT = 273
T_DEV = 512
NTOK = 4096
NDOC = 32
DOC_MOST = 2048
N_CTX = 8


def raised(values, own_key, source, target, blocks, factor):
    owner, partner = [(jnp.arange(values.shape[axis_at]) // (values.shape[axis_at] // blocks)).reshape([-1 if axis == axis_at else 1 for axis in range(values.ndim)]) for axis_at in (source, target)]
    chosen = jax.random.permutation(own_key, blocks)[partner]
    strong = (owner == chosen) | (owner == (partner + blocks // 2) % blocks)
    return jnp.where(strong, factor * values, values)


def block_scale(rng, dims, cuts, smallest, high):
    def one(dim, parts):
        steps = jax.random.uniform(jax.random.fold_in(jax.random.fold_in(rng, 6), dim), (parts,), jnp.float32, smallest / len(cuts), high / len(cuts))
        return jnp.repeat(jnp.exp(steps), dims[dim] // parts).reshape((-1,) + (1,) * (len(dims) - dim - 1))

    factor_of = one(*cuts[0])
    for cut in cuts[1:]:
        factor_of = factor_of * one(*cut)
    return factor_of


def profile(count, total, reach, skew):
    portions = [(1 << 20) // math.isqrt(grade ** skew) + 1 for grade in range(2, count + 1)]
    surplus, holding = total - reach - (count - 1), [1] * (count - 1)
    while surplus > 0:
        movable = [i for i in range(count - 1) if holding[i] < reach]
        mass, left = sum([portions[i] for i in movable]), surplus
        for i in movable:
            more = min(reach - holding[i], max(1, left * portions[i] // mass), surplus)
            holding[i] = holding[i] + more
            surplus = surplus - more
    return np.array([reach] + holding)


def ragged_sizes(own_key, amount, total, bound, slope):
    if amount == 2:
        one = jax.random.randint(own_key, (), max(1, total - bound), min(bound, total - 1) + 1)
        return jnp.stack([one, total - one])
    lengths = jnp.asarray(profile(amount, total, bound, slope), jnp.int32)
    pairs = (amount - 1) // 2
    source_of, taker = lengths[1:1 + 2 * pairs:2], lengths[2:2 + 2 * pairs:2]
    slack = jnp.minimum(source_of - 1, bound - taker)
    passed = jax.random.randint(jax.random.fold_in(own_key, 1), (pairs,), 0, 1 << 20) % (slack + 1)
    lengths = lengths.at[1:1 + 2 * pairs:2].set(source_of - passed).at[2:2 + 2 * pairs:2].set(taker + passed)
    return lengths[jax.random.permutation(jax.random.fold_in(own_key, 2), amount)]


def noise(key, dims, width, reach, pieces=(), kind=jnp.bfloat16):
    values = jax.random.normal(key, dims, jnp.float32) * width
    if len(pieces) > 0:
        values = block_scale(key, dims, pieces, -0.22, 0.18) * values
    return jnp.clip(values, min=-reach, max=reach).astype(kind)


def gaussian_with(stream_key, extent, deviation, limit, shards, heavy, held_as=jnp.bfloat16):
    entries = deviation * jax.random.normal(stream_key, extent, jnp.float32)
    if shards:
        entries = entries * block_scale(stream_key, extent, shards, -0.22, 0.18)
    return jnp.clip(raised(entries, jax.random.fold_in(stream_key, 3), *heavy), -limit, limit).astype(held_as)


def setup_inputs(seed: int = 0) -> dict:
    seeds = jax.random.split(jax.random.key(seed), 6)
    return {
        "query_key": noise(seeds[0], (NTOK, H * 2 * QK), 1.0, 6.0, ((0, 8), (1, 4))),
        "values": noise(seeds[1], (NTOK, H * HEAD), 1.0, 6.0, ((0, 8), (1, 4))),
        "out_grad": gaussian_with(seeds[2], (NTOK, D), 1.0, 6.0, ((0, 8), (1, 4)), (0, 1, 8, 2.0)),
        "out_weight": noise(seeds[3], (H * HEAD, D), (H * HEAD) ** -0.5, 0.09375, ((0, 4),)),
        "doc_lengths": ragged_sizes(seeds[4], NDOC, NTOK, DOC_MOST, 2).astype(jnp.int32),
    }


quad_scale = 0.25 / math.sqrt(2.0)
highest = lax.Precision.HIGHEST

def rounded(array):
    return lax.optimization_barrier(array.astype(jnp.bfloat16)).astype(jnp.float32)

def features(points):
    feat_width = points.shape[-1]
    constant = jnp.ones(points.shape[:-1] + (1,), jnp.float32)
    products = (points[..., :, None] * points[..., None, :]).reshape(points.shape[:-1] + (feat_width * feat_width,))
    return jnp.concatenate([constant, points * 0.5, products * quad_scale], axis=-1)

def feature_grad(grad_feat, points):
    feat_width = points.shape[-1]
    linear = grad_feat[..., 1:1 + feat_width] * 0.5
    square = grad_feat[..., 1 + feat_width:].reshape(points.shape[:-1] + (feat_width, feat_width))
    paired = square + jnp.swapaxes(square, -1, -2)
    return linear + quad_scale * lax.optimization_barrier(jnp.sum(paired * points[..., None, :], axis=-1))

def segment_ids(doc_lengths, positions):
    starts = (jnp.cumsum(doc_lengths, dtype=jnp.int32) - doc_lengths).astype(jnp.int32)
    return lax.optimization_barrier(jnp.sum((starts[None, :] <= positions[:, None]).astype(jnp.int32), axis=1)).astype(jnp.int32) - 1

def reference(query_key, values, out_grad, out_weight, doc_lengths):
    positions = jnp.arange(NTOK, dtype=jnp.int32)
    segment = segment_ids(doc_lengths, positions).reshape(N_CTX, T_DEV)
    previous = segment_ids(doc_lengths, positions - 1).reshape(N_CTX, T_DEV)
    open_before = previous[:, 0]
    open_after = segment[:, T_DEV - 1]
    restart = (open_after != open_before).astype(jnp.float32)
    carried = (segment == open_before[:, None]).astype(jnp.float32)
    ending = (segment == open_after[:, None]).astype(jnp.float32)
    paired = query_key.reshape(N_CTX, T_DEV, H, 2, QK).transpose(0, 2, 3, 1, 4)
    value_rows = values.reshape(N_CTX, T_DEV, H, HEAD).transpose(0, 2, 1, 3)
    upstream_all = jnp.dot(out_grad, out_weight.T, preferred_element_type=jnp.float32)
    upstream_all = upstream_all.reshape(N_CTX, T_DEV, H, HEAD).transpose(0, 2, 1, 3)

    def local_state(items):
        keys_part, value_part, ending_part = items
        key_feat = rounded(features(keys_part.astype(jnp.float32)))
        masked = key_feat * ending_part[None, :, None]
        state_part = jnp.einsum('htf,htd->hfd', masked, value_part.astype(jnp.float32), precision=highest)
        return (state_part, lax.optimization_barrier(jnp.sum(masked, axis=1)))
    state_local, norm_local = lax.map(local_state, (paired[:, :, 1], value_rows, ending))

    def forward_step(carry, items):
        state_part, norm_part, restart_part = items
        retained = 1.0 - restart_part
        return ((state_part + retained * carry[0], norm_part + retained * carry[1]), carry)
    zeros_state = (jnp.zeros((H, FEAT, HEAD), jnp.float32), jnp.zeros((H, FEAT), jnp.float32))
    unused, (state_in, norm_in) = lax.scan(forward_step, zeros_state, (state_local, norm_local, restart))

    def local_grads(items):
        queries, keys_all, value_part, upstream, segment_part, near_rows, state_part, norm_part = items
        places = jnp.arange(T_DEV, dtype=jnp.int32)
        query_float = queries.astype(jnp.float32)
        key_float = keys_all.astype(jnp.float32)
        value_float = value_part.astype(jnp.float32)
        query_feat = rounded(features(query_float))
        state_r = rounded(state_part)
        scores = jnp.einsum('hid,hjd->hij', query_float, key_float, precision=highest) * 0.25
        visible = (places[None, :] <= places[:, None]) & (segment_part[:, None] == segment_part[None, :])
        weight = jnp.where(visible[None], 1.0 + scores + 0.5 * scores * scores, 0.0)
        weight_r = rounded(weight)
        from_state = jnp.einsum('hif,hfd->hid', query_feat, state_r, precision=highest)
        numerator = jnp.einsum('hij,hjd->hid', weight_r, value_float, precision=highest) + near_rows[None, :, None] * from_state
        denominator = lax.optimization_barrier(jnp.sum(weight, axis=2)) + near_rows[None, :] * jnp.einsum('hif,hf->hi', query_feat, norm_part, precision=highest)
        attended = numerator / denominator[:, :, None]
        den_grad = -lax.optimization_barrier(jnp.sum(upstream * attended, axis=2)) / denominator
        num_float = rounded(upstream / denominator[:, :, None])
        mix_grad = jnp.einsum('hid,hjd->hij', num_float, value_float, precision=highest) + den_grad[:, :, None]
        score_grad = rounded(jnp.where(visible[None], mix_grad * (1.0 + scores), 0.0))
        value_grad = jnp.einsum('hij,hid->hjd', weight_r, num_float, precision=highest)
        key_grad = 0.25 * jnp.einsum('hij,hid->hjd', score_grad, query_float, precision=highest)
        feat_grad = near_rows[None, :, None] * (jnp.einsum('hid,hfd->hif', num_float, state_r, precision=highest) + den_grad[:, :, None] * norm_part[:, None, :])
        query_grad = 0.25 * jnp.einsum('hij,hjd->hid', score_grad, key_float, precision=highest) + feature_grad(feat_grad, query_float)
        near_feat = query_feat * near_rows[None, :, None]
        adj_part = jnp.einsum('hif,hid->hfd', near_feat, num_float, precision=highest)
        nadj_part = jnp.einsum('hif,hi->hf', near_feat, den_grad, precision=highest)
        return (attended.astype(jnp.bfloat16), query_grad.astype(jnp.bfloat16), key_grad, value_grad, adj_part, nadj_part)
    attended, query_grad, key_grad, value_grad, adj_local, nadj_local = lax.map(local_grads, (paired[:, :, 0], paired[:, :, 1], value_rows, upstream_all, segment, carried, state_in, norm_in))

    def backward_step(carry, items):
        adj_part, nadj_part, restart_part = items
        retained = 1.0 - restart_part
        return ((adj_part + retained * carry[0], nadj_part + retained * carry[1]), carry)
    unused, (adj_in, nadj_in) = lax.scan(backward_step, zeros_state, (adj_local, nadj_local, restart), reverse=True)

    def finish(items):
        keys_all, value_part, ending_part, key_part, value_part_grad, adj_part, nadj_part = items
        key_float = keys_all.astype(jnp.float32)
        key_feat = rounded(features(key_float))
        adj_r = rounded(adj_part)
        ending_col = ending_part[None, :, None]
        value_total = value_part_grad + ending_col * jnp.einsum('htf,hfd->htd', key_feat, adj_r, precision=highest)
        key_feat_grad = ending_col * (jnp.einsum('htd,hfd->htf', value_part.astype(jnp.float32), adj_r, precision=highest) + nadj_part[:, None, :])
        key_total = key_part + feature_grad(key_feat_grad, key_float)
        return (key_total.astype(jnp.bfloat16), value_total.astype(jnp.bfloat16))
    key_out, value_out = lax.map(finish, (paired[:, :, 1], value_rows, ending, key_grad, value_grad, adj_in, nadj_in))
    attended_flat = attended.transpose(0, 2, 1, 3).reshape(NTOK, H * HEAD)
    proj_grad = jnp.dot(attended_flat.T, out_grad, preferred_element_type=jnp.float32)
    qk_grad = jnp.stack([query_grad, key_out], axis=2).transpose(0, 3, 1, 2, 4).reshape(NTOK, H * 2 * QK)
    value_grad_out = value_out.transpose(0, 2, 1, 3).reshape(NTOK, H * HEAD)
    return (qk_grad, value_grad_out, proj_grad)
```

```python
import functools
import math

import jax
import jax.numpy as jnp
import numpy as np
from jax import lax
from jax.experimental import pallas as pl
from jax.experimental.pallas import tpu as pltpu
from jax.sharding import PartitionSpec as P

HEAD = 128
QK = 16
DOC_MOST = 2048

quad_scale = 0.25 / math.sqrt(2.0)

bf16 = jnp.bfloat16
f32 = jnp.float32
MESH = pl.DeviceIdType.MESH

PAIRS = [(a, b) for a in range(QK) for b in range(a, QK)]
FEAT = 160


def tables():
    left = np.zeros((FEAT, QK), np.float32)
    right = np.zeros((FEAT, QK), np.float32)
    cols = np.zeros((FEAT, 4), np.float32)
    cols[0, 0] = cols[0, 1] = cols[0, 2] = 1.0
    cols[:, 3] = 1.0
    for a in range(QK):
        left[1 + a, a] = 1.0
        cols[1 + a, 1] = 1.0
        cols[1 + a, 2] = 0.5
    for place, (a, b) in enumerate(PAIRS):
        left[1 + QK + place, a] = 1.0
        right[1 + QK + place, b] = 1.0
        cols[1 + QK + place, 2] = quad_scale
        cols[1 + QK + place, 3] = 1.0 if a == b else 2.0
    return left, right, cols


LEFT, RIGHT, COLS = tables()


def mm(a, b, ca, cb):
    return lax.dot_general(a, b, (((ca,), (cb,)), ((), ())), preferred_element_type=f32)


def split_rows(rows):
    high = rows.astype(bf16).astype(f32)
    place = lax.broadcasted_iota(jnp.int32, rows.shape, 0)
    return jnp.where(place == 0, high, jnp.where(place == 1, rows - high, 0.0)).astype(bf16)


def kernel(
    count,
    depth,
    docs_ref,
    qk_ref,
    v_ref,
    g_ref,
    w_ref,
    lcol_ref,
    rcol_ref,
    lrow_ref,
    rrow_ref,
    cols_ref,
    wrow_ref,
    qk_out,
    v_out,
    p_out,
    out_ref,
    wbuf,
    qkt,
    qkg,
    phiq,
    phik,
    mask_ref,
    wb_ref,
    y_ref,
    att_ref,
    up_ref,
    ng_ref,
    den_ref,
    dg_ref,
    rows_ref,
    st_ref,
    nin_ref,
    own,
    oth,
    pair,
    arr,
    nown,
    noth,
    npair,
    narr,
    vg_ref,
    acc,
    psend,
    precv,
    rbuf,
    pbuf,
    wsem,
    gsem,
    osem,
    ag_send,
    ag_recv,
    c_send,
    c_recv,
    p_ssem,
    p_rsem,
    s_ssem,
    s_rsem,
):
    tokens = qk_ref.shape[0]
    heads = v_ref.shape[1] // HEAD
    rows_all = heads * HEAD
    shard = g_ref.shape[1]
    chips = count // 2
    bits = chips.bit_length() - 1
    roots = chips // depth
    cw = shard // (2 * roots)
    half_t = tokens // 2
    half_r = rows_all // 2
    span = arr.shape[1]
    c = lax.axis_index("ctx")
    z = lax.axis_index("head")
    chip = c // 2
    core = c % 2
    other_core = 1 - core
    partner = 2 * chip + other_core
    chip_bit = [(chip // (1 << b)) % 2 for b in range(bits)]
    neighbour = [2 * (chip + (1 - 2 * chip_bit[b]) * (1 << b)) + core for b in range(bits)]

    barrier = pltpu.get_barrier_semaphore()

    met = [(None, {"ctx": partner, "head": z})]
    met += [(z > 0, {"ctx": c, "head": z - 1}), (z < depth - 1, {"ctx": c, "head": z + 1})]
    met += [(None, {"ctx": neighbour[b], "head": z}) for b in range(bits) if (1 << b) > span]
    for k in range(1, span + 1):
        met += [
            (chip >= k, {"ctx": c - 2 * k, "head": z}),
            (chip + k < chips, {"ctx": c + 2 * k, "head": z}),
        ]
    peers = 0
    for cond, where in met:

        def greet(where=where):
            pl.semaphore_signal(barrier, inc=1, device_id=where, device_id_type=MESH)

        if cond is None:
            greet()
            peers = peers + 1
        else:
            pl.when(cond)(greet)
            peers = peers + cond.astype(jnp.int32)
    pl.semaphore_wait(barrier, peers)

    def piece(n):
        if n == 0:
            return z
        k = (n + 1) // 2
        inner = z - k if n % 2 else z + k
        low_side = 1 - (2 * z + 1) // depth
        lesser = low_side * z + (1 - low_side) * (depth - 1 - z)
        outer = low_side * n + (1 - low_side) * (depth - 1 - n)
        beyond = (n - 2 * lesser - 1 + 4 * depth) // (4 * depth)
        return (1 - beyond) * inner + beyond * outer

    def slot(way, k, level):
        if k == 0:
            return 0
        low_side = 1 - (2 * level + 1) // depth
        lesser = low_side * level + (1 - low_side) * (depth - 1 - level)
        beyond = (k - lesser - 1 + 2 * depth) // (2 * depth)
        return (1 - beyond) * (2 * k - 1 + way) + beyond * (lesser + k)

    def part_rows(part):
        return pl.ds(part * half_t, half_t)

    def ag(way, k, part):
        to = z + 1 - 2 * way
        if k == 0:
            src = g_ref.at[part_rows(part), :]
        else:
            src = out_ref.at[slot(way, k, z), part_rows(part), :]
        return pltpu.make_async_remote_copy(
            src_ref=src,
            dst_ref=out_ref.at[slot(way, k + 1, to), part_rows(part), :],
            send_sem=ag_send.at[way, k, part],
            recv_sem=ag_recv.at[way, k, part],
            device_id={"ctx": c, "head": to},
            device_id_type=MESH,
        )

    def ag_arrival(way, k, part):
        came = out_ref.at[slot(way, k, z), part_rows(part), :]
        return pltpu.make_async_remote_copy(
            src_ref=came,
            dst_ref=came,
            send_sem=ag_send.at[way, k, part],
            recv_sem=ag_recv.at[way, k - 1, part],
            device_id={"ctx": c, "head": z - 1 + 2 * way},
            device_id_type=MESH,
        )

    def ag_cond(way, k):
        if way == 0:
            return (z >= k) & (z < depth - 1)
        return (z + k <= depth - 1) & (z > 0)

    def ag_has(way, k):
        return z >= k if way == 0 else z + k <= depth - 1

    for part in range(2):
        for way in range(2):
            pl.when(ag_cond(way, 0))(lambda way=way, part=part: ag(way, 0, part).start())

    def arrive(k, part):
        for way in range(2):

            @pl.when(ag_has(way, k))
            def _(way=way):
                ag_arrival(way, k, part).wait_recv()

            if k < depth - 1:
                pl.when(ag_cond(way, k))(lambda way=way: ag(way, k, part).start())

    own_copy = pltpu.make_async_copy(g_ref, out_ref.at[0], gsem)
    own_copy.start()

    def w_copy(n):
        at = pl.multiple_of(piece(n) * shard, shard)
        return pltpu.make_async_copy(w_ref.at[:, pl.ds(at, shard)], wbuf.at[n % 2], wsem.at[n % 2])

    w_copy(0).start()
    if depth > 1:
        w_copy(1).start()

    places_row = c * tokens + lax.broadcasted_iota(jnp.int32, (1, tokens), 1)
    places_col = c * tokens + lax.broadcasted_iota(jnp.int32, (tokens, 1), 0)
    low_edge, edge_count = -2 * (span - 1), 4 * span - 1
    bounds = [(2 * chip + low_edge + e) * tokens - 1 for e in range(edge_count)]

    def doc(d, carry):
        start, row, col, counts = carry
        row = row + (start <= places_row).astype(jnp.int32)
        col = col + (start <= places_col).astype(jnp.int32)
        counts = tuple(
            n + jnp.where(start <= bound, 1, 0) for n, bound in zip(counts, bounds)
        )
        return start + docs_ref[d], row, col, counts

    _, seg_row, seg_col, counts = lax.fori_loop(
        0,
        docs_ref.shape[0],
        doc,
        (
            jnp.int32(0),
            jnp.zeros((1, tokens), jnp.int32),
            jnp.zeros((tokens, 1), jnp.int32),
            tuple(jnp.int32(0) for _ in range(edge_count)),
        ),
    )

    def edges(offset):
        return counts[offset - low_edge]

    def keep(offset):
        block = 2 * chip + offset
        inside = (block >= 0) & (block < count)
        return jnp.where(inside, jnp.where(edges(offset) == edges(offset + 1), 1.0, 0.0), 0.0)

    before = jnp.where(core == 0, edges(0), edges(1))
    after = jnp.where(core == 0, edges(1), edges(2))
    rows_ref[0] = jnp.broadcast_to((seg_row == before).astype(f32), (8, tokens))
    rows_ref[1] = jnp.broadcast_to((seg_row == after).astype(f32), (8, tokens))
    for r in range(tokens // 128):
        at = slice(r * 128, (r + 1) * 128)
        jj = r * 128 + lax.broadcasted_iota(jnp.int32, (128, tokens), 0)
        ii = lax.broadcasted_iota(jnp.int32, (128, tokens), 1)
        same = seg_col[at] == seg_row
        mask_ref[at, :] = jnp.where(jj <= ii, jnp.where(same, 1.0, 0.0), 0.0)

    qkt[...] = qk_ref[...].astype(f32).T.astype(bf16)

    def head_rows(h):
        return pl.ds(pl.multiple_of(h * HEAD, HEAD), HEAD)

    def query(h):
        return qkt[pl.ds(pl.multiple_of(h * 2 * QK, QK), QK), :]

    def key(h):
        return qkt[pl.ds(pl.multiple_of(h * 2 * QK + QK, QK), QK), :]

    def feature_factors(points):
        first = mm(lcol_ref[...], points, 1, 0) + cols_ref[:, 0:1]
        second = mm(rcol_ref[...], points, 1, 0) + cols_ref[:, 1:2]
        return first, second

    def feature_grad(grad, first, second):
        scaled = grad * cols_ref[:, 2:3]
        return mm(lrow_ref[...], (scaled * second).astype(bf16), 1, 0) + mm(
            rrow_ref[...], (scaled * first).astype(bf16), 1, 0
        )

    def each_head(first, last, body):
        @pl.loop(first, last)
        def _(h):
            body(h)

    def carry_copies(way, k):
        to = partner if k == 0 else c + 2 * k * (1 - 2 * way)
        src, nsrc = (own, nown) if k == 0 else (pair, npair)
        dst, ndst = (
            (oth.at[way], noth.at[way]) if k == 0 else (arr.at[way, k - 1], narr.at[way, k - 1])
        )
        return [
            pltpu.make_async_remote_copy(
                src_ref=s.at[way],
                dst_ref=d,
                send_sem=c_send.at[way, k, i],
                recv_sem=c_recv.at[way, k, i],
                device_id={"ctx": to, "head": z},
                device_id_type=MESH,
            )
            for i, (s, d) in enumerate(((src, dst), (nsrc, ndst)))
        ]

    def onward(way, k):
        return chip + k < chips if way == 0 else chip >= k

    def behind(way, k):
        return chip >= k if way == 0 else chip + k < chips

    def start_all(copies):
        for copy in copies:
            copy.start()

    def carry_pair(way):
        for copy in carry_copies(way, 0):
            copy.wait_recv()
        keep_near = keep(1 - way)
        early = core == way
        mine = jnp.where(early, keep_near, 1.0)
        theirs = jnp.where(early, 1.0, keep_near)

        def one(h):
            pair[way, h] = (mine * own[way, h].astype(f32) + theirs * oth[way, h].astype(f32)).astype(bf16)
            npair[way, h] = mine * nown[way, h] + theirs * noth[way, h]

        each_head(0, heads, one)
        for k in range(1, span + 1):
            pl.when(onward(way, k))(lambda k=k: start_all(carry_copies(way, k)))

    def carry_arrive(way):
        for k in range(1, span + 1):

            @pl.when(behind(way, k))
            def _(k=k):
                for copy in carry_copies(way, k):
                    copy.wait_recv()

    def carry_total(way, h):
        early = core == way
        near = jnp.where(early, 0.0, 1.0)
        far = jnp.where(early, 1.0, keep(way))
        total, ntotal, through = 0.0, 0.0, far
        for k in range(1, span + 1):
            if k > 1:
                base = 2 * (k - 1) * (2 * way - 1)
                through = through * keep(base) * keep(base + 1)
            there = behind(way, k)
            total = total + through * jnp.where(there, arr[way, k - 1, h].astype(f32), 0.0)
            ntotal = ntotal + through * jnp.where(there, narr[way, k - 1, h], 0.0)
        return near * oth[way, h].astype(f32) + total, near * noth[way, h] + ntotal

    carried_row = rows_ref[0, 0:1]
    ending_row = rows_ref[1, 0:1]
    ones8 = jnp.ones((8, tokens), bf16)

    def features(h):
        first, second = feature_factors(key(h))
        feat = (first * second * cols_ref[:, 2:3] * ending_row).astype(bf16)
        phik[h] = feat
        own[0, h] = (mm(feat, v_ref[:, head_rows(h)], 1, 0) * cols_ref[:, 3:4]).astype(bf16)
        nown[0, h] = mm(ones8, feat, 1, 1) * wrow_ref[...]
        first, second = feature_factors(query(h))
        phiq[h] = (first * second * cols_ref[:, 2:3] * carried_row).astype(bf16)

    each_head(0, heads, features)
    start_all(carry_copies(0, 0))

    blocks = [(slice(0, half_t), half_t), (slice(half_t, tokens), tokens)]

    def scores_of(h, at, upto):
        return mm(key(h)[:, :upto], query(h)[:, at] * bf16(0.25), 0, 0)

    def attend(h):
        for at, upto in blocks:
            s = scores_of(h, at, upto)
            weight = ((0.5 * s + 1.0) * s + 1.0) * mask_ref[:upto, at]
            weight_b = weight.astype(bf16)
            wb_ref[h, :upto, at] = weight_b
            den_ref[h, :, at] = jnp.broadcast_to(
                jnp.sum(weight, axis=0, keepdims=True), (8, half_t)
            )
            y_ref[h, :, at] = mm(v_ref[:upto, head_rows(h)], weight_b, 0, 0)

    third = max(1, heads // 4)
    each_head(0, third, attend)
    carry_pair(0)
    each_head(third, heads // 2, attend)
    if depth > 1:
        arrive(1, 0)
    each_head(heads // 2, heads, attend)
    carry_arrive(0)

    def finish_forward(h):
        state, norm = carry_total(0, h)
        state_b = state.astype(bf16)
        st_ref[h] = state_b
        nin_ref[h] = norm
        feat = phiq[h]
        from_state = mm(state_b, feat, 0, 0)
        from_norm = jnp.sum(mm(split_rows(norm), feat, 1, 0), axis=0, keepdims=True)
        inverse = 1.0 / (den_ref[h, 0:1] + from_norm)
        den_ref[h] = jnp.broadcast_to(inverse, (8, tokens))
        y = (y_ref[h] + from_state) * inverse
        y_ref[h] = y
        att_ref[head_rows(h), :] = y.astype(bf16)

    each_head(0, heads, finish_forward)
    own_copy.wait()

    row_block = min(256, rows_all)
    blocks_of_rows = rows_all // row_block

    def columns(j, which):
        return slice((2 * j + which) * cw, (2 * j + which + 1) * cw)

    def partner_copy(n):
        return pltpu.make_async_remote_copy(
            src_ref=psend.at[n],
            dst_ref=precv.at[n],
            send_sem=p_ssem.at[n],
            recv_sem=p_rsem.at[n],
            device_id={"ctx": partner, "head": z},
            device_id_type=MESH,
        )

    def product(n):
        def halves(mine):
            @pl.loop(0, blocks_of_rows)
            def _(b):
                at = pl.ds(pl.multiple_of(b * row_block, row_block), row_block)
                for j in range(roots):
                    psend[n, at, j * cw : (j + 1) * cw] = mm(
                        att_ref[at, :], out_ref[n, :, columns(j, 1 - mine)], 1, 0
                    ).astype(bf16)

            partner_copy(n).start()

            @pl.loop(0, blocks_of_rows)
            def _(b):
                at = pl.ds(pl.multiple_of(b * row_block, row_block), row_block)
                for j in range(roots):
                    acc[n, at, j * cw : (j + 1) * cw] = mm(
                        att_ref[at, :], out_ref[n, :, columns(j, mine)], 1, 0
                    )

        for mine in range(2):
            pl.when(core == mine)(lambda mine=mine: halves(mine))

    def upstream(n):
        w_copy(n).wait()

        @pl.loop(0, blocks_of_rows)
        def _(b):
            at = pl.ds(pl.multiple_of(b * row_block, row_block), row_block)
            part = mm(wbuf[n % 2, at, :], out_ref[n], 1, 1)
            up_ref[at, :] = part if n == 0 else up_ref[at, :] + part

        if n + 2 < depth:
            w_copy(n + 2).start()

    orders = [list(range(bits))[::-1], list(range(bits))]

    def relative(n, j, b):
        root = piece(n) * roots + j
        return (chip_bit[b] + (root // (1 << b)) % 2) % 2

    def taking_part(n, j, flow, stage):
        live = None
        for b in orders[flow][:stage]:
            here = relative(n, j, b) == 0
            live = here if live is None else live & here
        return live

    def both(a, b):
        return b if a is None else a & b

    def flow_rows(flow):
        return pl.ds(flow * half_r, half_r)

    def flow_columns(j):
        return pl.ds(j * cw, cw)

    def stage_copy(n, j, flow, stage):
        b = orders[flow][stage]
        return pltpu.make_async_remote_copy(
            src_ref=psend.at[n, flow_rows(flow), flow_columns(j)],
            dst_ref=rbuf.at[n, stage, flow_rows(flow), flow_columns(j)],
            send_sem=s_ssem.at[n, flow, j],
            recv_sem=s_rsem.at[n, stage, flow, j],
            device_id={"ctx": neighbour[b], "head": z},
            device_id_type=MESH,
        )

    def result_copy(j, flow):
        return pltpu.make_async_copy(
            pbuf.at[flow_rows(flow), :], p_out.at[flow_rows(flow), :], osem.at[flow]
        )

    def tree(n, step):
        if step == 0:
            partner_copy(n).wait()
        for flow in (0, 1) if step % 2 == 0 else (1, 0):
            for j in range(roots):
                at, cols = flow_rows(flow), slice(j * cw, (j + 1) * cw)
                came = None
                if step == 0:
                    acc[n, at, cols] = acc[n, at, cols] + precv[n, at, cols].astype(f32)
                else:
                    live = taking_part(n, j, flow, step - 1)
                    came = both(live, relative(n, j, orders[flow][step - 1]) == 0)

                    @pl.when(came)
                    def _():
                        stage_copy(n, j, flow, step - 1).wait_recv()
                        total = acc[n, at, cols] + rbuf[n, step - 1, at, cols].astype(f32)
                        if step == bits:
                            pbuf[at, :] = total
                            result_copy(j, flow).start()
                        else:
                            acc[n, at, cols] = total

                if step < bits:
                    live = taking_part(n, j, flow, step)

                    @pl.when(both(live, relative(n, j, orders[flow][step]) == 1))
                    def _():
                        psend[n, at, cols] = acc[n, at, cols].astype(bf16)
                        stage_copy(n, j, flow, step).start()

    for n in range(depth - 1):
        if n > 1:
            arrive(n, 0)
            arrive(n, 1)
        product(n)
        upstream(n)
        tree(n, 0)
        if n == 0:
            arrive(1, 1)
        for k in range(1, bits + 1):
            if n - k >= 0:
                tree(n - k, k)
    last = depth - 1
    if last > 1:
        arrive(last, 0)
        arrive(last, 1)
    product(last)
    upstream(last)

    def start_backward(h):
        up = up_ref[head_rows(h), :]
        inverse = den_ref[h, 0:1]
        den_grad = -jnp.sum(up * y_ref[h], axis=0, keepdims=True) * inverse
        num_grad = (up * inverse).astype(bf16)
        ng_ref[h] = num_grad
        den_rows = jnp.broadcast_to(den_grad, (8, tokens))
        dg_ref[h] = den_rows
        feat = phiq[h]
        own[1, h] = (mm(feat, num_grad, 1, 1) * cols_ref[:, 3:4]).astype(bf16)
        nadj = jnp.sum(mm(split_rows(den_rows), feat, 1, 1), axis=0, keepdims=True)
        nown[1, h] = jnp.broadcast_to(nadj, (8, FEAT)) * wrow_ref[...]

    each_head(0, heads, start_backward)
    start_all(carry_copies(1, 0))
    tree(last, 0)
    for k in range(1, bits + 1):
        if last - k >= 0:
            tree(last - k, k)
    carry_pair(1)

    def key_rows(h):
        return pl.ds(pl.multiple_of(h * 2 * QK + QK, QK), QK)

    def query_rows(h):
        return pl.ds(pl.multiple_of(h * 2 * QK, QK), QK)

    def outer(rows, dense):
        place = lax.broadcasted_iota(jnp.int32, rows.shape, 0)
        high = rows.astype(bf16).astype(f32)
        left = jnp.where(place == 2, rows - high, jnp.where(place < 2, high, 0.0)).astype(bf16)
        place = lax.broadcasted_iota(jnp.int32, dense.shape, 0)
        high = dense.astype(bf16).astype(f32)
        right = jnp.where(place == 1, dense - high, high).astype(bf16)
        return mm(left, right, 0, 0)

    def attention_grad(h):
        value_part = []
        key_part = []
        for at, upto in blocks:
            q4 = query(h)[:, at] * bf16(0.25)
            grad = ng_ref[h, :, at]
            s = mm(key(h)[:, :upto], q4, 0, 0)
            mix = mm(v_ref[:upto, head_rows(h)], grad, 1, 0) + dg_ref[h, 0:1, at]
            score_grad = (mix * (1.0 + s) * mask_ref[:upto, at]).astype(bf16)
            qkg[query_rows(h), at] = mm(key(h)[:, :upto] * bf16(0.25), score_grad, 1, 0)
            key_part.append(mm(score_grad, q4, 1, 1))
            value_part.append(mm(wb_ref[h, :upto, at], grad, 1, 1))
        vg_ref[h, :half_t] = value_part[0] + value_part[1][:half_t]
        vg_ref[h, half_t:] = value_part[1][half_t:]
        key_sum = jnp.concatenate([key_part[0] + key_part[1][:half_t], key_part[1][half_t:]], axis=0)
        qkg[key_rows(h), :] = key_sum.T
        grad = mm(st_ref[h], ng_ref[h], 1, 0) + outer(nin_ref[h], dg_ref[h])
        first, second = feature_factors(query(h))
        qkg[query_rows(h), :] += feature_grad(grad, first, second) * carried_row

    cut = [heads * (r + 1) // (bits + 1) for r in range(bits)]
    low = 0
    for r in range(1, bits + 1):
        each_head(low, cut[r - 1], attention_grad)
        low = cut[r - 1]
        for k in range(r, bits + 1):
            if last + r - k >= 0:
                tree(last + r - k, k)
    each_head(low, heads, attention_grad)

    carry_arrive(1)

    def finish(h):
        adjoint, nadj = carry_total(1, h)
        adjoint_b = adjoint.astype(bf16)
        feat = phik[h]
        v_out[:, head_rows(h)] = (vg_ref[h] + mm(feat, adjoint_b, 0, 0)).astype(bf16)
        grad = mm(adjoint_b, v_ref[:, head_rows(h)], 1, 1) + mm(split_rows(nadj), ones8, 0, 0)
        first, second = feature_factors(key(h))
        qkg[key_rows(h), :] += feature_grad(grad, first, second) * ending_row

    each_head(0, heads, finish)
    qk_out[...] = qkg[...].T.astype(bf16)

    for part in range(2):
        for way in range(2):
            for k in range(depth - 1):
                pl.when(ag_cond(way, k))(
                    lambda way=way, k=k, part=part: ag(way, k, part).wait_send()
                )
    for way in range(2):
        for copy in carry_copies(way, 0):
            copy.wait_send()
        for k in range(1, span + 1):

            @pl.when(onward(way, k))
            def _(way=way, k=k):
                for copy in carry_copies(way, k):
                    copy.wait_send()

    for n in range(depth):
        for j in range(roots):
            for flow in range(2):
                for stage in range(bits):
                    sends = both(
                        taking_part(n, j, flow, stage), relative(n, j, orders[flow][stage]) == 1
                    )
                    pl.when(sends)(
                        lambda n=n, j=j, flow=flow, stage=stage: stage_copy(
                            n, j, flow, stage
                        ).wait_send()
                    )
    for flow in range(2):
        result_copy(0, flow).wait()


def on_device(query_key, values, out_grad, out_weight, doc_lengths):
    tokens = query_key.shape[0]
    rows_all = out_weight.shape[0]
    heads = rows_all // HEAD
    shard = out_grad.shape[1]
    count = lax.axis_size("ctx")
    depth = lax.axis_size("head")
    chips = count // 2
    bits = chips.bit_length() - 1
    roots = chips // depth
    width = out_weight.shape[1] // count
    span = (DOC_MOST // tokens + 1) // 2
    whole = pl.BlockSpec(memory_space=pltpu.VMEM)
    hbm = pl.BlockSpec(memory_space=pl.ANY)
    vmem = pltpu.VMEM
    dma = pltpu.SemaphoreType.DMA
    scratch = [
        vmem((depth, tokens, shard), bf16),
        vmem((2, rows_all, shard), bf16),
        vmem((2 * QK * heads, tokens), bf16),
        vmem((2 * QK * heads, tokens), f32),
        vmem((heads, FEAT, tokens), bf16),
        vmem((heads, FEAT, tokens), bf16),
        vmem((tokens, tokens), f32),
        vmem((heads, tokens, tokens), bf16),
        vmem((heads, HEAD, tokens), f32),
        vmem((rows_all, tokens), bf16),
        vmem((rows_all, tokens), f32),
        vmem((heads, HEAD, tokens), bf16),
        vmem((heads, 8, tokens), f32),
        vmem((heads, 8, tokens), f32),
        vmem((2, 8, tokens), f32),
        vmem((heads, FEAT, HEAD), bf16),
        vmem((heads, 8, FEAT), f32),
        vmem((2, heads, FEAT, HEAD), bf16),
        vmem((2, heads, FEAT, HEAD), bf16),
        vmem((2, heads, FEAT, HEAD), bf16),
        vmem((2, span, heads, FEAT, HEAD), bf16),
        vmem((2, heads, 8, FEAT), f32),
        vmem((2, heads, 8, FEAT), f32),
        vmem((2, heads, 8, FEAT), f32),
        vmem((2, span, heads, 8, FEAT), f32),
        vmem((heads, tokens, HEAD), f32),
        vmem((depth, rows_all, roots * width), f32),
        vmem((depth, rows_all, roots * width), bf16),
        vmem((depth, rows_all, roots * width), bf16),
        vmem((depth, bits, rows_all, roots * width), bf16),
        vmem((rows_all, width), f32),
        dma((2,)),
        dma,
        dma((2,)),
        dma((2, depth, 2)),
        dma((2, depth, 2)),
        dma((2, span + 1, 2)),
        dma((2, span + 1, 2)),
        dma((depth,)),
        dma((depth,)),
        dma((depth, 2, roots)),
        dma((depth, bits, 2, roots)),
    ]
    return pl.pallas_call(
        functools.partial(kernel, count, depth),
        name="step",
        out_shape=(
            jax.ShapeDtypeStruct(query_key.shape, bf16),
            jax.ShapeDtypeStruct(values.shape, bf16),
            jax.ShapeDtypeStruct((rows_all, width), f32),
        ),
        in_specs=[
            pl.BlockSpec(memory_space=pltpu.SMEM),
            whole,
            whole,
            hbm,
            hbm,
            whole,
            whole,
            whole,
            whole,
            whole,
            whole,
        ],
        out_specs=(whole, whole, hbm),
        scratch_shapes=scratch,
        compiler_params=pltpu.CompilerParams(
            collective_id=0, has_side_effects=True, vmem_limit_bytes=67_043_328
        ),
    )(
        doc_lengths,
        query_key,
        values,
        out_grad,
        out_weight,
        jnp.asarray(LEFT, bf16),
        jnp.asarray(RIGHT, bf16),
        jnp.asarray(LEFT.T, bf16),
        jnp.asarray(RIGHT.T, bf16),
        jnp.asarray(COLS),
        jnp.asarray(np.broadcast_to(COLS[:, 3][None], (8, FEAT)).copy()),
    )


def solution(mesh):
    placed = (P("ctx", "head"), P("ctx", "head"), P("ctx", "head"), P("head", None), P())
    return jax.shard_map(
        on_device,
        mesh=mesh,
        in_specs=placed,
        out_specs=(P("ctx", "head"), P("ctx", "head"), P("head", "ctx")),
        check_vma=False,
    )
```

```python
import functools
import math

import jax
import jax.numpy as jnp
import numpy as np
from jax import lax
from jax.experimental import pallas as pl
from jax.experimental.pallas import tpu as pltpu
from jax.sharding import PartitionSpec as P

HEAD = 128
QK = 16
DOC_MOST = 2048
LAG = 2

quad_scale = 0.25 / math.sqrt(2.0)

bf16 = jnp.bfloat16
f32 = jnp.float32
MESH = pl.DeviceIdType.MESH

PAIRS = [(a, b) for a in range(QK) for b in range(a, QK)]
FEAT = 160


def tables():
    left = np.zeros((FEAT, QK), np.float32)
    right = np.zeros((FEAT, QK), np.float32)
    cols = np.zeros((FEAT, 4), np.float32)
    cols[0, 0] = cols[0, 1] = cols[0, 2] = 1.0
    cols[:, 3] = 1.0
    for a in range(QK):
        left[1 + a, a] = 1.0
        cols[1 + a, 1] = 1.0
        cols[1 + a, 2] = 0.5
    for place, (a, b) in enumerate(PAIRS):
        left[1 + QK + place, a] = 1.0
        right[1 + QK + place, b] = 1.0
        cols[1 + QK + place, 2] = quad_scale
        cols[1 + QK + place, 3] = 1.0 if a == b else 2.0
    return left, right, cols


LEFT, RIGHT, COLS = tables()


def mm(a, b, ca, cb):
    return lax.dot_general(a, b, (((ca,), (cb,)), ((), ())), preferred_element_type=f32)


def split_rows(rows):
    high = rows.astype(bf16).astype(f32)
    place = lax.broadcasted_iota(jnp.int32, rows.shape, 0)
    return jnp.where(place == 0, high, jnp.where(place == 1, rows - high, 0.0)).astype(bf16)


def kernel(
    count,
    depth,
    docs_ref,
    qk_hbm,
    v_hbm,
    g_ref,
    w_ref,
    lcol_ref,
    rcol_ref,
    lrow_ref,
    rrow_ref,
    cols_ref,
    wrow_ref,
    qk_out,
    v_out,
    p_out,
    qk_ref,
    v_ref,
    v_held,
    out_ref,
    wbuf,
    qkt,
    qkg,
    phiq,
    phik,
    mask_ref,
    slope_ref,
    wb_ref,
    y_ref,
    att_ref,
    up_ref,
    ng_ref,
    den_ref,
    dg_ref,
    rows_ref,
    st_ref,
    own,
    oth,
    pair,
    arr,
    tot,
    nown,
    noth,
    npair,
    narr,
    ntot,
    vg_ref,
    acc,
    psend,
    precv,
    rbuf,
    pbuf,
    isem,
    wsem,
    gsem,
    osem,
    ag_send,
    ag_recv,
    c_send,
    c_recv,
    p_ssem,
    p_rsem,
    s_ssem,
    s_rsem,
):
    tokens = qk_hbm.shape[0]
    heads = v_hbm.shape[1] // HEAD
    rows_all = heads * HEAD
    shard = g_ref.shape[1]
    chips = count // 2
    bits = chips.bit_length() - 1
    roots = chips // depth
    cw = shard // (2 * roots)
    half_t = tokens // 2
    half_h = heads // 2
    shares = acc.shape[0] // depth
    cg = cw // shares
    half_r = rows_all // 2
    span = arr.shape[1]
    c = lax.axis_index("ctx")
    z = lax.axis_index("head")
    chip = c // 2
    core = c % 2
    other_core = 1 - core
    partner = 2 * chip + other_core
    chip_bit = [(chip // (1 << b)) % 2 for b in range(bits)]
    neighbour = [2 * (chip + (1 - 2 * chip_bit[b]) * (1 << b)) + core for b in range(bits)]

    barrier = pltpu.get_barrier_semaphore()

    met = [(None, {"ctx": partner, "head": z})]
    met += [(z > 0, {"ctx": c, "head": z - 1}), (z < depth - 1, {"ctx": c, "head": z + 1})]
    met += [(None, {"ctx": neighbour[b], "head": z}) for b in range(bits) if (1 << b) > span]
    for k in range(1, span + 1):
        met += [
            (chip >= k, {"ctx": c - 2 * k, "head": z}),
            (chip + k < chips, {"ctx": c + 2 * k, "head": z}),
        ]
    peers = 0
    for cond, where in met:

        def greet(where=where):
            pl.semaphore_signal(barrier, inc=1, device_id=where, device_id_type=MESH)

        if cond is None:
            greet()
            peers = peers + 1
        else:
            pl.when(cond)(greet)
            peers = peers + cond.astype(jnp.int32)
    pl.semaphore_wait(barrier, peers)

    def piece(n):
        if n == 0:
            return z
        k = (n + 1) // 2
        inner = z - k if n % 2 else z + k
        low_side = 1 - (2 * z + 1) // depth
        lesser = low_side * z + (1 - low_side) * (depth - 1 - z)
        outer = low_side * n + (1 - low_side) * (depth - 1 - n)
        beyond = (n - 2 * lesser - 1 + 4 * depth) // (4 * depth)
        return (1 - beyond) * inner + beyond * outer

    def slot(way, k, level):
        if k == 0:
            return 0
        low_side = 1 - (2 * level + 1) // depth
        lesser = low_side * level + (1 - low_side) * (depth - 1 - level)
        beyond = (k - lesser - 1 + 2 * depth) // (2 * depth)
        return (1 - beyond) * (2 * k - 1 + way) + beyond * (lesser + k)

    parts = [(g, j, which) for g in range(shares) for j in range(roots) for which in range(2)]

    def part_slice(part):
        g, j, which = parts[part]
        return pl.ds((2 * j + which) * cw + g * cg, cg)

    def held_at(place, part):
        g, j, which = parts[part]
        return out_ref.at[place, g, :, pl.ds((2 * j + which) * cg, cg)]

    def ag(way, k, part):
        to = z + 1 - 2 * way
        if k == 0:
            src = g_ref.at[:, part_slice(part)]
        else:
            src = held_at(slot(way, k, z), part)
        return pltpu.make_async_remote_copy(
            src_ref=src,
            dst_ref=held_at(slot(way, k + 1, to), part),
            send_sem=ag_send.at[way, k, part],
            recv_sem=ag_recv.at[way, k, part],
            device_id={"ctx": c, "head": to},
            device_id_type=MESH,
        )

    def ag_arrival(way, k, part):
        came = held_at(slot(way, k, z), part)
        return pltpu.make_async_remote_copy(
            src_ref=came,
            dst_ref=came,
            send_sem=ag_send.at[way, k, part],
            recv_sem=ag_recv.at[way, k - 1, part],
            device_id={"ctx": c, "head": z - 1 + 2 * way},
            device_id_type=MESH,
        )

    def ag_cond(way, k):
        if way == 0:
            return (z >= k) & (z < depth - 1)
        return (z + k <= depth - 1) & (z > 0)

    def ag_has(way, k):
        return z >= k if way == 0 else z + k <= depth - 1

    for part in range(len(parts)):
        for way in range(2):
            pl.when(ag_cond(way, 0))(lambda way=way, part=part: ag(way, 0, part).start())

    def arrive(k, share):
        for part in range(len(parts)):
            for way in range(2):
                if parts[part][0] == share:

                    @pl.when(ag_has(way, k))
                    def _(way=way, part=part):
                        ag_arrival(way, k, part).wait_recv()

                    if k < depth - 1:
                        pl.when(ag_cond(way, k))(
                            lambda way=way, part=part: ag(way, k, part).start()
                        )

    own_copies = [
        pltpu.make_async_copy(g_ref.at[:, part_slice(part)], held_at(0, part), gsem.at[part])
        for part in range(len(parts))
    ]
    for copy in own_copies:
        copy.start()

    def w_copies(n):
        at = piece(n) * shard
        copies = []
        for part, (g, j, which) in enumerate(parts):
            start = pl.multiple_of(at + ((2 * j + which) * cw + g * cg), cg)
            copies.append(
                pltpu.make_async_copy(
                    w_ref.at[:, pl.ds(start, cg)],
                    wbuf.at[n % 2, g, :, pl.ds((2 * j + which) * cg, cg)],
                    wsem.at[n % 2, part],
                )
            )
        return copies

    def start_all(copies):
        for copy in copies:
            copy.start()

    for n in range(min(2, depth)):
        start_all(w_copies(n))

    inputs = [
        pltpu.make_async_copy(qk_hbm, qk_ref, isem.at[0]),
        pltpu.make_async_copy(v_hbm, v_ref, isem.at[1]),
    ]
    start_all(inputs)

    places_row = c * tokens + lax.broadcasted_iota(jnp.int32, (1, tokens), 1)
    places_col = c * tokens + lax.broadcasted_iota(jnp.int32, (tokens, 1), 0)
    low_edge, edge_count = -2 * (span - 1), 4 * span - 1
    bounds = [(2 * chip + low_edge + e) * tokens - 1 for e in range(edge_count)]

    def doc(d, carry):
        start, row, col, counts = carry
        row = row + (start <= places_row).astype(jnp.int32)
        col = col + (start <= places_col).astype(jnp.int32)
        counts = tuple(
            n + jnp.where(start <= bound, 1, 0) for n, bound in zip(counts, bounds)
        )
        return start + docs_ref[d], row, col, counts

    _, seg_row, seg_col, counts = lax.fori_loop(
        0,
        docs_ref.shape[0],
        doc,
        (
            jnp.int32(0),
            jnp.zeros((1, tokens), jnp.int32),
            jnp.zeros((tokens, 1), jnp.int32),
            tuple(jnp.int32(0) for _ in range(edge_count)),
        ),
    )

    def edges(offset):
        return counts[offset - low_edge]

    def keep(offset):
        block = 2 * chip + offset
        inside = (block >= 0) & (block < count)
        return jnp.where(inside, jnp.where(edges(offset) == edges(offset + 1), 1.0, 0.0), 0.0)

    before = jnp.where(core == 0, edges(0), edges(1))
    after = jnp.where(core == 0, edges(1), edges(2))
    rows_ref[0] = jnp.broadcast_to((seg_row == before).astype(f32), (8, tokens))
    rows_ref[1] = jnp.broadcast_to((seg_row == after).astype(f32), (8, tokens))
    for r in range(tokens // 128):
        at = slice(r * 128, (r + 1) * 128)
        jj = r * 128 + lax.broadcasted_iota(jnp.int32, (128, tokens), 0)
        ii = lax.broadcasted_iota(jnp.int32, (128, tokens), 1)
        same = seg_col[at] == seg_row
        mask_ref[at, :] = jnp.where(jj <= ii, jnp.where(same, 1.0, 0.0), 0.0)

    for copy in inputs:
        copy.wait()
    qkt[...] = qk_ref[...].astype(f32).T.astype(bf16)

    def head_rows(h):
        return pl.ds(pl.multiple_of(h * HEAD, HEAD), HEAD)

    def query(h):
        return qkt[pl.ds(pl.multiple_of(h * 2 * QK, QK), QK), :]

    def key(h):
        return qkt[pl.ds(pl.multiple_of(h * 2 * QK + QK, QK), QK), :]

    def feature_factors(points):
        first = mm(lcol_ref[...], points, 1, 0) + cols_ref[:, 0:1]
        second = mm(rcol_ref[...], points, 1, 0) + cols_ref[:, 1:2]
        return first, second

    def feature_grad(grad, first, second):
        scaled = grad * cols_ref[:, 2:3]
        return mm(lrow_ref[...], (scaled * second).astype(bf16), 1, 0) + mm(
            rrow_ref[...], (scaled * first).astype(bf16), 1, 0
        )

    def each_head(first, last, body):
        @pl.loop(first, last)
        def _(h):
            body(h)

    def my_heads():
        return pl.ds(core * half_h, half_h)

    def carry_copies(way, k):
        to = c + 2 * k * (1 - 2 * way) if k > 0 else partner
        if k == 0:
            moves = [(own.at[way], oth.at[way]), (nown.at[way], noth.at[way])]
        elif k > 0:
            moves = [(pair.at[way], arr.at[way, k - 1]), (npair.at[way], narr.at[way, k - 1])]
        else:
            moves = [(tot.at[way, my_heads()], tot.at[way, my_heads()])]
        at = k if k >= 0 else span + 1
        return [
            pltpu.make_async_remote_copy(
                src_ref=src,
                dst_ref=dst,
                send_sem=c_send.at[way, at, i],
                recv_sem=c_recv.at[way, at, i],
                device_id={"ctx": to, "head": z},
                device_id_type=MESH,
            )
            for i, (src, dst) in enumerate(moves)
        ]

    def total_arrival(way):
        came = tot.at[way, pl.ds(other_core * half_h, half_h)]
        return pltpu.make_async_remote_copy(
            src_ref=came,
            dst_ref=came,
            send_sem=c_send.at[way, span + 1, 0],
            recv_sem=c_recv.at[way, span + 1, 0],
            device_id={"ctx": partner, "head": z},
            device_id_type=MESH,
        )

    def onward(way, k):
        return chip + k < chips if way == 0 else chip >= k

    def behind(way, k):
        return chip >= k if way == 0 else chip + k < chips

    def carry_pair(way):
        for copy in carry_copies(way, 0):
            copy.wait_recv()
        keep_near = keep(1 - way)
        early = core == way
        mine = jnp.where(early, keep_near, 1.0)
        theirs = jnp.where(early, 1.0, keep_near)

        @pl.loop(0, half_h)
        def _(i):
            h = core * half_h + i
            pair[way, i] = (mine * own[way, h].astype(f32) + theirs * oth[way, h].astype(f32)).astype(bf16)

        npair[way] = mine * nown[way] + theirs * noth[way]
        for k in range(1, span + 1):
            pl.when(onward(way, k))(lambda k=k: start_all(carry_copies(way, k)))

    def carry_arrive(way):
        for k in range(1, span + 1):

            @pl.when(behind(way, k))
            def _(k=k):
                for copy in carry_copies(way, k):
                    copy.wait_recv()

        through = [jnp.float32(1.0)]
        for k in range(2, span + 1):
            base = 2 * (k - 1) * (2 * way - 1)
            through.append(through[-1] * keep(base) * keep(base + 1))

        def weighed(stack, index):
            total = 0.0
            for k in range(1, span + 1):
                came = jnp.where(behind(way, k), stack[(way, k - 1) + index].astype(f32), 0.0)
                total = total + through[k - 1] * came
            return total

        @pl.loop(0, half_h)
        def _(i):
            tot[way, core * half_h + i] = weighed(arr, (i,)).astype(bf16)

        start_all(carry_copies(way, -1))
        near, far = carry_shares(way)
        ntot[way] = near * noth[way] + far * weighed(narr, ())

    def carry_shares(way):
        early = core == way
        return jnp.where(early, 0.0, 1.0), jnp.where(early, 1.0, keep(way))

    def carry_total(way, h):
        near, far = carry_shares(way)
        norm = jnp.broadcast_to(ntot[way, pl.ds(h, 1), :], (8, FEAT))
        return near * oth[way, h].astype(f32) + far * tot[way, h].astype(f32), norm

    carried_row = rows_ref[0, 0:1]
    ending_row = rows_ref[1, 0:1]
    ones8 = jnp.ones((8, tokens), bf16)

    def features(h):
        first, second = feature_factors(key(h))
        feat = (first * second * cols_ref[:, 2:3] * ending_row).astype(bf16)
        phik[h] = feat
        own[0, h] = (mm(feat, v_ref[:, head_rows(h)], 1, 0) * cols_ref[:, 3:4]).astype(bf16)
        nown[0, pl.ds(h, 1), :] = (mm(ones8, feat, 1, 1) * wrow_ref[...])[0:1]
        first, second = feature_factors(query(h))
        phiq[h] = (first * second * cols_ref[:, 2:3] * carried_row).astype(bf16)

    each_head(0, heads, features)
    start_all(carry_copies(0, 0))

    blocks = [(slice(0, half_t), half_t), (slice(half_t, tokens), tokens)]

    def scores_of(h, at, upto):
        return mm(key(h)[:, :upto], query(h)[:, at] * bf16(0.25), 0, 0)

    def attend(h):
        for at, upto in blocks:
            s = scores_of(h, at, upto)
            slope_ref[h, :upto, at] = (1.0 + s) * mask_ref[:upto, at]
            weight = ((0.5 * s + 1.0) * s + 1.0) * mask_ref[:upto, at]
            weight_b = weight.astype(bf16)
            wb_ref[h, :upto, at] = weight_b
            den_ref[h, :, at] = jnp.broadcast_to(
                jnp.sum(weight, axis=0, keepdims=True), (8, half_t)
            )
            y_ref[h, :, at] = mm(v_ref[:upto, head_rows(h)], weight_b, 0, 0)

    each_head(0, heads // 4, attend)
    carry_pair(0)
    each_head(heads // 4, heads // 2, attend)
    arrive(1, 0)
    each_head(heads // 2, 3 * heads // 4, attend)
    carry_arrive(0)
    each_head(3 * heads // 4, heads, attend)
    total_arrival(0).wait_recv()

    def finish_forward(h):
        state, norm = carry_total(0, h)
        state_b = state.astype(bf16)
        st_ref[h] = state_b
        feat = phiq[h]
        from_state = mm(state_b, feat, 0, 0)
        from_norm = jnp.sum(mm(split_rows(norm), feat, 1, 0), axis=0, keepdims=True)
        inverse = 1.0 / (den_ref[h, 0:1] + from_norm)
        den_ref[h] = jnp.broadcast_to(inverse, (8, tokens))
        y = (y_ref[h] + from_state) * inverse
        y_ref[h] = y
        att_ref[head_rows(h), :] = y.astype(bf16)

    each_head(0, heads, finish_forward)
    for copy in own_copies:
        copy.wait()

    row_block = min(256, rows_all)
    blocks_of_rows = rows_all // row_block

    def partner_copy(m):
        return pltpu.make_async_remote_copy(
            src_ref=psend.at[m],
            dst_ref=precv.at[m],
            send_sem=p_ssem.at[m],
            recv_sem=p_rsem.at[m],
            device_id={"ctx": partner, "head": z},
            device_id_type=MESH,
        )

    def product(m):
        n, g = m // shares, m % shares

        @pl.loop(0, blocks_of_rows)
        def _(b):
            at = pl.ds(pl.multiple_of(b * row_block, row_block), row_block)
            both_cores = mm(att_ref[at, :], out_ref[n, g], 1, 0)
            for mine in range(2):

                @pl.when(core == mine)
                def _():
                    for j in range(roots):
                        to = slice(j * cg, (j + 1) * cg)
                        theirs = (2 * j + 1 - mine) * cg
                        ours = (2 * j + mine) * cg
                        psend[m, at, to] = both_cores[:, theirs : theirs + cg].astype(bf16)
                        acc[m, at, to] = both_cores[:, ours : ours + cg]

        partner_copy(m).start()

    def upstream(m):
        n, g = m // shares, m % shares
        if g == 0:
            for copy in w_copies(n):
                copy.wait()

        @pl.loop(0, blocks_of_rows)
        def _(b):
            at = pl.ds(pl.multiple_of(b * row_block, row_block), row_block)
            one = mm(wbuf[n % 2, g, at, :], out_ref[n, g], 1, 1)
            up_ref[at, :] = one if m == 0 else up_ref[at, :] + one

        if g == shares - 1 and n + 2 < depth:
            start_all(w_copies(n + 2))

    if bits == 2:
        flows = [
            [({one: 1, two: 0}, two), ({one: 1, two: 1}, one), ({one: 0, two: 1}, two)]
            for one, two in ((0, 1), (1, 0))
        ]
    else:
        flows = []
        for order in (list(range(bits))[::-1], list(range(bits))):
            done = [dict.fromkeys(order[:stage], 0) for stage in range(bits)]
            flows.append([({**done[stage], b: 1}, b) for stage, b in enumerate(order)])
    stages = len(flows[0])

    def relative(m, j, b):
        root = piece(m // shares) * roots + j
        return (chip_bit[b] + (root // (1 << b)) % 2) % 2

    def matches(m, j, pattern):
        live = None
        for b, value in pattern.items():
            here = relative(m, j, b) == value
            live = here if live is None else live & here
        return live

    def sends(m, j, flow, stage):
        return matches(m, j, flows[flow][stage][0])

    def receives(m, j, flow, stage):
        pattern, b = flows[flow][stage]
        return matches(m, j, {**pattern, b: 1 - pattern[b]})

    def inbox(stage):
        return stage % rbuf.shape[1]

    def flow_rows(flow):
        return pl.ds(flow * half_r, half_r)

    def flow_columns(j):
        return pl.ds(j * cg, cg)

    def stage_copy(m, j, flow, stage):
        b = flows[flow][stage][1]
        return pltpu.make_async_remote_copy(
            src_ref=psend.at[m, flow_rows(flow), flow_columns(j)],
            dst_ref=rbuf.at[m, inbox(stage), flow_rows(flow), flow_columns(j)],
            send_sem=s_ssem.at[m, flow, j],
            recv_sem=s_rsem.at[m, inbox(stage), flow, j],
            device_id={"ctx": neighbour[b], "head": z},
            device_id_type=MESH,
        )

    def result_copy(g, flow):
        return pltpu.make_async_copy(
            pbuf.at[g, flow_rows(flow), :],
            p_out.at[flow_rows(flow), pl.ds(g * cg, cg)],
            osem.at[g, flow],
        )

    def tree(m, step):
        if step == 0:
            partner_copy(m).wait()
        for flow in range(2):
            for j in range(roots):
                at, cols = flow_rows(flow), slice(j * cg, (j + 1) * cg)
                if step == 0:
                    acc[m, at, cols] = acc[m, at, cols] + precv[m, at, cols].astype(f32)
                else:

                    @pl.when(receives(m, j, flow, step - 1))
                    def _():
                        stage_copy(m, j, flow, step - 1).wait_recv()
                        total = acc[m, at, cols] + rbuf[m, inbox(step - 1), at, cols].astype(f32)
                        if step == stages:
                            pbuf[m % shares, at, :] = total
                            result_copy(m % shares, flow).start()
                        else:
                            acc[m, at, cols] = total

                if step < stages:

                    @pl.when(sends(m, j, flow, step))
                    def _():
                        psend[m, at, cols] = acc[m, at, cols].astype(bf16)
                        stage_copy(m, j, flow, step).start()

    last = depth * shares - 1

    def trees(m):
        for step in range(stages + 1):
            if 0 <= m - LAG * step <= last:
                tree(m - LAG * step, step)

    for m in range(last):
        if m >= 2 * shares:
            arrive(m // shares, m % shares)
        if 0 < m < shares:
            arrive(1, m)
        product(m)
        upstream(m)
        trees(m)
    arrive(last // shares, last % shares)
    product(last)
    upstream(last)

    def start_backward(h):
        up = up_ref[head_rows(h), :]
        inverse = den_ref[h, 0:1]
        den_grad = -jnp.sum(up * y_ref[h], axis=0, keepdims=True) * inverse
        num_grad = (up * inverse).astype(bf16)
        ng_ref[h] = num_grad
        den_rows = jnp.broadcast_to(den_grad, (8, tokens))
        dg_ref[h] = den_rows
        feat = phiq[h]
        own[1, h] = (mm(feat, num_grad, 1, 1) * cols_ref[:, 3:4]).astype(bf16)
        nadj = jnp.sum(mm(split_rows(den_rows), feat, 1, 1), axis=0, keepdims=True)
        nown[1, pl.ds(h, 1), :] = nadj * wrow_ref[0:1]

    each_head(0, heads, start_backward)
    start_all(carry_copies(1, 0))
    trees(last)
    carry_pair(1)

    def key_rows(h):
        return pl.ds(pl.multiple_of(h * 2 * QK + QK, QK), QK)

    def query_rows(h):
        return pl.ds(pl.multiple_of(h * 2 * QK, QK), QK)

    def outer(rows, dense):
        place = lax.broadcasted_iota(jnp.int32, rows.shape, 0)
        high = rows.astype(bf16).astype(f32)
        left = jnp.where(place == 2, rows - high, jnp.where(place < 2, high, 0.0)).astype(bf16)
        place = lax.broadcasted_iota(jnp.int32, dense.shape, 0)
        high = dense.astype(bf16).astype(f32)
        right = jnp.where(place == 1, dense - high, high).astype(bf16)
        return mm(left, right, 0, 0)

    def attention_grad(h):
        value_part = []
        key_part = []
        for at, upto in blocks:
            q4 = query(h)[:, at] * bf16(0.25)
            grad = ng_ref[h, :, at]
            mix = mm(v_ref[:upto, head_rows(h)], grad, 1, 0) + dg_ref[h, 0:1, at]
            score_grad = (mix * slope_ref[h, :upto, at]).astype(bf16)
            qkg[query_rows(h), at] = mm(key(h)[:, :upto] * bf16(0.25), score_grad, 1, 0)
            key_part.append(mm(score_grad, q4, 1, 1))
            value_part.append(mm(wb_ref[h, :upto, at], grad, 1, 1))
        vg_ref[h, :half_t] = value_part[0] + value_part[1][:half_t]
        vg_ref[h, half_t:] = value_part[1][half_t:]
        key_sum = jnp.concatenate([key_part[0] + key_part[1][:half_t], key_part[1][half_t:]], axis=0)
        qkg[key_rows(h), :] = key_sum.T
        grad = mm(st_ref[h], ng_ref[h], 1, 0) + outer(jnp.broadcast_to(ntot[0, pl.ds(h, 1), :], (8, FEAT)), dg_ref[h])
        first, second = feature_factors(query(h))
        qkg[query_rows(h), :] += feature_grad(grad, first, second) * carried_row

    rounds = LAG * stages
    steps = 2 * heads

    def remaining(at):
        for r in range(at * rounds // steps, (at + 1) * rounds // steps):
            trees(last + 1 + r)

    for h in range(heads):
        each_head(h, h + 1, attention_grad)
        remaining(h)
        if h == heads // 2:
            carry_arrive(1)

    total_arrival(1).wait_recv()

    def finish(h):
        adjoint, nadj = carry_total(1, h)
        adjoint_b = adjoint.astype(bf16)
        feat = phik[h]
        v_held[:, head_rows(h)] = (vg_ref[h] + mm(feat, adjoint_b, 0, 0)).astype(bf16)
        grad = mm(adjoint_b, v_ref[:, head_rows(h)], 1, 1) + mm(split_rows(nadj), ones8, 0, 0)
        first, second = feature_factors(key(h))
        qkg[key_rows(h), :] += feature_grad(grad, first, second) * ending_row

    for h in range(heads):
        each_head(h, h + 1, finish)
        remaining(heads + h)
    qk_ref[...] = qkg[...].T.astype(bf16)
    outputs = [
        pltpu.make_async_copy(qk_ref, qk_out, isem.at[0]),
        pltpu.make_async_copy(v_held, v_out, isem.at[1]),
    ]
    start_all(outputs)

    for part in range(len(parts)):
        for way in range(2):
            for k in range(depth - 1):
                pl.when(ag_cond(way, k))(
                    lambda way=way, k=k, part=part: ag(way, k, part).wait_send()
                )
    for way in range(2):
        for copy in carry_copies(way, 0) + carry_copies(way, -1):
            copy.wait_send()
        for k in range(1, span + 1):

            @pl.when(onward(way, k))
            def _(way=way, k=k):
                for copy in carry_copies(way, k):
                    copy.wait_send()

    for m in range(last + 1):
        for j in range(roots):
            for flow in range(2):
                for stage in range(stages):
                    pl.when(sends(m, j, flow, stage))(
                        lambda m=m, j=j, flow=flow, stage=stage: stage_copy(
                            m, j, flow, stage
                        ).wait_send()
                    )
    for g in range(shares):
        for flow in range(2):
            result_copy(g, flow).wait()
    for copy in outputs:
        copy.wait()


def hand_on_kernel(cuts, *refs):
    count = len(cuts)
    sources, targets, held = refs[:count], refs[count : 2 * count], refs[2 * count : 3 * count]
    sem_in, sem_out = refs[3 * count :]
    moves = []
    for n, cut in enumerate(cuts):
        size = sources[n].shape[0] // cut
        for at in range(cut):
            rows = pl.ds(at * size, size)
            place = len(moves)
            moves.append(
                (
                    pltpu.make_async_copy(sources[n].at[rows], held[n].at[rows], sem_in.at[place]),
                    pltpu.make_async_copy(held[n].at[rows], targets[n].at[rows], sem_out.at[place]),
                )
            )
    for come, _ in moves:
        come.start()
    for come, go in moves:
        come.wait()
        go.start()
    for _, go in moves:
        go.wait()


def hand_on(*arrays):
    cuts = [max(1, a.size * a.dtype.itemsize >> 18) for a in arrays]
    hbm = pl.BlockSpec(memory_space=pl.ANY)
    return pl.pallas_call(
        functools.partial(hand_on_kernel, cuts),
        name="hand_on",
        out_shape=tuple(jax.ShapeDtypeStruct(a.shape, a.dtype) for a in arrays),
        in_specs=[hbm] * len(arrays),
        out_specs=(hbm,) * len(arrays),
        scratch_shapes=[pltpu.VMEM(a.shape, a.dtype) for a in arrays]
        + [pltpu.SemaphoreType.DMA((sum(cuts),)), pltpu.SemaphoreType.DMA((sum(cuts),))],
    )(*arrays)


def on_device(query_key, values, out_grad, out_weight, doc_lengths):
    tokens = query_key.shape[0]
    rows_all = out_weight.shape[0]
    heads = rows_all // HEAD
    count = lax.axis_size("ctx")
    depth = lax.axis_size("head")
    chips = count // 2
    bits = chips.bit_length() - 1
    roots = chips // depth
    width = out_weight.shape[1] // count
    span = (DOC_MOST // tokens + 1) // 2
    shares = max(1, min(4, width // 128))
    inboxes = 1 if bits == 2 else bits
    wide = roots * width // shares
    parts = 2 * roots * shares
    pieces = depth * shares
    whole = pl.BlockSpec(memory_space=pltpu.VMEM)
    hbm = pl.BlockSpec(memory_space=pl.ANY)
    vmem = pltpu.VMEM
    dma = pltpu.SemaphoreType.DMA
    scratch = [
        vmem(query_key.shape, bf16),
        vmem(values.shape, bf16),
        vmem(values.shape, bf16),
        vmem((depth, shares, tokens, 2 * wide), bf16),
        vmem((2, shares, rows_all, 2 * wide), bf16),
        vmem((2 * QK * heads, tokens), bf16),
        vmem((2 * QK * heads, tokens), f32),
        vmem((heads, FEAT, tokens), bf16),
        vmem((heads, FEAT, tokens), bf16),
        vmem((tokens, tokens), f32),
        vmem((heads, tokens, tokens), f32),
        vmem((heads, tokens, tokens), bf16),
        vmem((heads, HEAD, tokens), f32),
        vmem((rows_all, tokens), bf16),
        vmem((rows_all, tokens), f32),
        vmem((heads, HEAD, tokens), bf16),
        vmem((heads, 8, tokens), f32),
        vmem((heads, 8, tokens), f32),
        vmem((2, 8, tokens), f32),
        vmem((heads, FEAT, HEAD), bf16),
        vmem((2, heads, FEAT, HEAD), bf16),
        vmem((2, heads, FEAT, HEAD), bf16),
        vmem((2, heads // 2, FEAT, HEAD), bf16),
        vmem((2, span, heads // 2, FEAT, HEAD), bf16),
        vmem((2, heads, FEAT, HEAD), bf16),
        vmem((2, heads, FEAT), f32),
        vmem((2, heads, FEAT), f32),
        vmem((2, heads, FEAT), f32),
        vmem((2, span, heads, FEAT), f32),
        vmem((2, heads, FEAT), f32),
        vmem((heads, tokens, HEAD), f32),
        vmem((pieces, rows_all, wide), f32),
        vmem((pieces, rows_all, wide), bf16),
        vmem((pieces, rows_all, wide), bf16),
        vmem((pieces, inboxes, rows_all, wide), bf16),
        vmem((shares, rows_all, width // shares), f32),
        dma((2,)),
        dma((2, parts)),
        dma((parts,)),
        dma((shares, 2)),
        dma((2, depth, parts)),
        dma((2, depth, parts)),
        dma((2, span + 2, 2)),
        dma((2, span + 2, 2)),
        dma((pieces,)),
        dma((pieces,)),
        dma((pieces, 2, roots)),
        dma((pieces, inboxes, 2, roots)),
    ]
    results = pl.pallas_call(
        functools.partial(kernel, count, depth),
        name="step",
        out_shape=(
            jax.ShapeDtypeStruct(query_key.shape, bf16),
            jax.ShapeDtypeStruct(values.shape, bf16),
            jax.ShapeDtypeStruct((rows_all, width), f32),
        ),
        in_specs=[
            pl.BlockSpec(memory_space=pltpu.SMEM),
            hbm,
            hbm,
            hbm,
            hbm,
            whole,
            whole,
            whole,
            whole,
            whole,
            whole,
        ],
        out_specs=(hbm, hbm, hbm),
        scratch_shapes=scratch,
        compiler_params=pltpu.CompilerParams(
            collective_id=0, has_side_effects=True, vmem_limit_bytes=67_043_328
        ),
    )(
        doc_lengths,
        query_key,
        values,
        out_grad,
        out_weight,
        jnp.asarray(LEFT, bf16),
        jnp.asarray(RIGHT, bf16),
        jnp.asarray(LEFT.T, bf16),
        jnp.asarray(RIGHT.T, bf16),
        jnp.asarray(COLS),
        jnp.asarray(np.broadcast_to(COLS[:, 3][None], (8, FEAT)).copy()),
    )
    return hand_on(*results)


def solution(mesh):
    placed = (P("ctx", "head"), P("ctx", "head"), P("ctx", "head"), P("head", None), P())
    return jax.shard_map(
        on_device,
        mesh=mesh,
        in_specs=placed,
        out_specs=(P("ctx", "head"), P("ctx", "head"), P("head", "ctx")),
        check_vma=False,
    )
```

```python
import functools
import math

import jax
import jax.numpy as jnp
import numpy as np
from jax import lax
from jax.experimental import pallas as pl
from jax.experimental.pallas import tpu as pltpu
from jax.sharding import PartitionSpec as P

HEAD = 128
QK = 16
DOC_MOST = 2048
LAG = 2

quad_scale = 0.25 / math.sqrt(2.0)

bf16 = jnp.bfloat16
f32 = jnp.float32
MESH = pl.DeviceIdType.MESH

PAIRS = [(a, b) for a in range(QK) for b in range(a, QK)]
FEAT = 160


def tables():
    left = np.zeros((FEAT, QK), np.float32)
    right = np.zeros((FEAT, QK), np.float32)
    cols = np.zeros((FEAT, 4), np.float32)
    cols[0, 0] = cols[0, 1] = cols[0, 2] = 1.0
    cols[:, 3] = 1.0
    for a in range(QK):
        left[1 + a, a] = 1.0
        cols[1 + a, 1] = 1.0
        cols[1 + a, 2] = 0.5
    for place, (a, b) in enumerate(PAIRS):
        left[1 + QK + place, a] = 1.0
        right[1 + QK + place, b] = 1.0
        cols[1 + QK + place, 2] = quad_scale
        cols[1 + QK + place, 3] = 1.0 if a == b else 2.0
    return left, right, cols


LEFT, RIGHT, COLS = tables()


def mm(a, b, ca, cb):
    return lax.dot_general(a, b, (((ca,), (cb,)), ((), ())), preferred_element_type=f32)


def split_rows(rows):
    high = rows.astype(bf16).astype(f32)
    place = lax.broadcasted_iota(jnp.int32, rows.shape, 0)
    return jnp.where(place == 0, high, jnp.where(place == 1, rows - high, 0.0)).astype(bf16)


def kernel(
    count,
    depth,
    docs_ref,
    qk_hbm,
    v_hbm,
    g_ref,
    w_ref,
    lcol_ref,
    rcol_ref,
    lrow_ref,
    rrow_ref,
    cols_ref,
    wrow_ref,
    qk_out,
    v_out,
    p_out,
    qk_ref,
    v_ref,
    v_held,
    out_ref,
    wbuf,
    qkt,
    qkg,
    phiq,
    phik,
    mask_ref,
    slope_ref,
    wb_ref,
    y_ref,
    att_ref,
    up_ref,
    ng_ref,
    den_ref,
    dg_ref,
    rows_ref,
    st_ref,
    own,
    oth,
    pair,
    arr,
    tot,
    nown,
    noth,
    npair,
    narr,
    ntot,
    vg_ref,
    acc,
    psend,
    precv,
    rbuf,
    pbuf,
    isem,
    wsem,
    gsem,
    osem,
    ag_send,
    ag_recv,
    c_send,
    c_recv,
    p_ssem,
    p_rsem,
    s_ssem,
    s_rsem,
):
    tokens = qk_hbm.shape[0]
    heads = v_hbm.shape[1] // HEAD
    rows_all = heads * HEAD
    shard = g_ref.shape[1]
    chips = count // 2
    bits = chips.bit_length() - 1
    roots = chips // depth
    cw = shard // (2 * roots)
    half_t = tokens // 2
    half_h = heads // 2
    shares = acc.shape[0] // depth
    cg = cw // shares
    half_r = rows_all // 2
    span = arr.shape[1]
    c = lax.axis_index("ctx")
    z = lax.axis_index("head")
    chip = c // 2
    core = c % 2
    other_core = 1 - core
    partner = 2 * chip + other_core
    chip_bit = [(chip // (1 << b)) % 2 for b in range(bits)]
    neighbour = [2 * (chip + (1 - 2 * chip_bit[b]) * (1 << b)) + core for b in range(bits)]

    barrier = pltpu.get_barrier_semaphore()

    met = [(None, {"ctx": partner, "head": z})]
    met += [(z > 0, {"ctx": c, "head": z - 1}), (z < depth - 1, {"ctx": c, "head": z + 1})]
    met += [(None, {"ctx": neighbour[b], "head": z}) for b in range(bits) if (1 << b) > span]
    for k in range(1, span + 1):
        met += [
            (chip >= k, {"ctx": c - 2 * k, "head": z}),
            (chip + k < chips, {"ctx": c + 2 * k, "head": z}),
        ]
    peers = 0
    for cond, where in met:

        def greet(where=where):
            pl.semaphore_signal(barrier, inc=1, device_id=where, device_id_type=MESH)

        if cond is None:
            greet()
            peers = peers + 1
        else:
            pl.when(cond)(greet)
            peers = peers + cond.astype(jnp.int32)
    pl.semaphore_wait(barrier, peers)

    def piece(n):
        if n == 0:
            return z
        k = (n + 1) // 2
        inner = z - k if n % 2 else z + k
        low_side = 1 - (2 * z + 1) // depth
        lesser = low_side * z + (1 - low_side) * (depth - 1 - z)
        outer = low_side * n + (1 - low_side) * (depth - 1 - n)
        beyond = (n - 2 * lesser - 1 + 4 * depth) // (4 * depth)
        return (1 - beyond) * inner + beyond * outer

    def slot(way, k, level):
        if k == 0:
            return 0
        low_side = 1 - (2 * level + 1) // depth
        lesser = low_side * level + (1 - low_side) * (depth - 1 - level)
        beyond = (k - lesser - 1 + 2 * depth) // (2 * depth)
        return (1 - beyond) * (2 * k - 1 + way) + beyond * (lesser + k)

    parts = [(g, j, which) for g in range(shares) for j in range(roots) for which in range(2)]

    def part_slice(part):
        g, j, which = parts[part]
        return pl.ds((2 * j + which) * cw + g * cg, cg)

    def held_at(place, part):
        g, j, which = parts[part]
        return out_ref.at[place, g, :, pl.ds((2 * j + which) * cg, cg)]

    def ag(way, k, part):
        to = z + 1 - 2 * way
        if k == 0:
            src = g_ref.at[:, part_slice(part)]
        else:
            src = held_at(slot(way, k, z), part)
        return pltpu.make_async_remote_copy(
            src_ref=src,
            dst_ref=held_at(slot(way, k + 1, to), part),
            send_sem=ag_send.at[way, k, part],
            recv_sem=ag_recv.at[way, k, part],
            device_id={"ctx": c, "head": to},
            device_id_type=MESH,
        )

    def ag_arrival(way, k, part):
        came = held_at(slot(way, k, z), part)
        return pltpu.make_async_remote_copy(
            src_ref=came,
            dst_ref=came,
            send_sem=ag_send.at[way, k, part],
            recv_sem=ag_recv.at[way, k - 1, part],
            device_id={"ctx": c, "head": z - 1 + 2 * way},
            device_id_type=MESH,
        )

    def ag_cond(way, k):
        if way == 0:
            return (z >= k) & (z < depth - 1)
        return (z + k <= depth - 1) & (z > 0)

    def ag_has(way, k):
        return z >= k if way == 0 else z + k <= depth - 1

    for part in range(len(parts)):
        for way in range(2):
            pl.when(ag_cond(way, 0))(lambda way=way, part=part: ag(way, 0, part).start())

    def arrive(k, share):
        for part in range(len(parts)):
            for way in range(2):
                if parts[part][0] == share:

                    @pl.when(ag_has(way, k))
                    def _(way=way, part=part):
                        ag_arrival(way, k, part).wait_recv()

                    if k < depth - 1:
                        pl.when(ag_cond(way, k))(
                            lambda way=way, part=part: ag(way, k, part).start()
                        )

    own_copies = [
        pltpu.make_async_copy(g_ref.at[:, part_slice(part)], held_at(0, part), gsem.at[part])
        for part in range(len(parts))
    ]
    for copy in own_copies:
        copy.start()

    def w_copies(n):
        at = piece(n) * shard
        copies = []
        for part, (g, j, which) in enumerate(parts):
            start = pl.multiple_of(at + ((2 * j + which) * cw + g * cg), cg)
            copies.append(
                pltpu.make_async_copy(
                    w_ref.at[:, pl.ds(start, cg)],
                    wbuf.at[n % 2, g, :, pl.ds((2 * j + which) * cg, cg)],
                    wsem.at[n % 2, part],
                )
            )
        return copies

    def start_all(copies):
        for copy in copies:
            copy.start()

    for n in range(min(2, depth)):
        start_all(w_copies(n))

    inputs = [
        pltpu.make_async_copy(qk_hbm, qk_ref, isem.at[0]),
        pltpu.make_async_copy(v_hbm, v_ref, isem.at[1]),
    ]
    start_all(inputs)

    places_row = c * tokens + lax.broadcasted_iota(jnp.int32, (1, tokens), 1)
    places_col = c * tokens + lax.broadcasted_iota(jnp.int32, (tokens, 1), 0)
    low_edge, edge_count = -2 * (span - 1), 4 * span - 1
    bounds = [(2 * chip + low_edge + e) * tokens - 1 for e in range(edge_count)]

    def doc(d, carry):
        start, row, col, counts = carry
        row = row + (start <= places_row).astype(jnp.int32)
        col = col + (start <= places_col).astype(jnp.int32)
        counts = tuple(
            n + jnp.where(start <= bound, 1, 0) for n, bound in zip(counts, bounds)
        )
        return start + docs_ref[d], row, col, counts

    _, seg_row, seg_col, counts = lax.fori_loop(
        0,
        docs_ref.shape[0],
        doc,
        (
            jnp.int32(0),
            jnp.zeros((1, tokens), jnp.int32),
            jnp.zeros((tokens, 1), jnp.int32),
            tuple(jnp.int32(0) for _ in range(edge_count)),
        ),
    )

    def edges(offset):
        return counts[offset - low_edge]

    def keep(offset):
        block = 2 * chip + offset
        inside = (block >= 0) & (block < count)
        return jnp.where(inside, jnp.where(edges(offset) == edges(offset + 1), 1.0, 0.0), 0.0)

    before = jnp.where(core == 0, edges(0), edges(1))
    after = jnp.where(core == 0, edges(1), edges(2))
    rows_ref[0] = jnp.broadcast_to((seg_row == before).astype(f32), (8, tokens))
    rows_ref[1] = jnp.broadcast_to((seg_row == after).astype(f32), (8, tokens))
    for r in range(tokens // 128):
        at = slice(r * 128, (r + 1) * 128)
        jj = r * 128 + lax.broadcasted_iota(jnp.int32, (128, tokens), 0)
        ii = lax.broadcasted_iota(jnp.int32, (128, tokens), 1)
        same = seg_col[at] == seg_row
        mask_ref[at, :] = jnp.where(jj <= ii, jnp.where(same, 1.0, 0.0), 0.0)

    for copy in inputs:
        copy.wait()
    qkt[...] = qk_ref[...].astype(f32).T.astype(bf16)

    def head_rows(h):
        return pl.ds(pl.multiple_of(h * HEAD, HEAD), HEAD)

    def query(h):
        return qkt[pl.ds(pl.multiple_of(h * 2 * QK, QK), QK), :]

    def key(h):
        return qkt[pl.ds(pl.multiple_of(h * 2 * QK + QK, QK), QK), :]

    def feature_factors(points):
        first = mm(lcol_ref[...], points, 1, 0) + cols_ref[:, 0:1]
        second = mm(rcol_ref[...], points, 1, 0) + cols_ref[:, 1:2]
        return first, second

    def feature_grad(grad, first, second):
        scaled = grad * cols_ref[:, 2:3]
        return mm(lrow_ref[...], (scaled * second).astype(bf16), 1, 0) + mm(
            rrow_ref[...], (scaled * first).astype(bf16), 1, 0
        )

    def each_head(first, last, body):
        @pl.loop(first, last)
        def _(h):
            body(h)

    def my_heads():
        return pl.ds(core * half_h, half_h)

    def carry_copies(way, k):
        to = c + 2 * k * (1 - 2 * way) if k > 0 else partner
        if k == 0:
            moves = [(own.at[way], oth.at[way]), (nown.at[way], noth.at[way])]
        elif k > 0:
            moves = [(pair.at[way], arr.at[way, k - 1]), (npair.at[way], narr.at[way, k - 1])]
        else:
            moves = [(tot.at[way, my_heads()], tot.at[way, my_heads()])]
        at = k if k >= 0 else span + 1
        return [
            pltpu.make_async_remote_copy(
                src_ref=src,
                dst_ref=dst,
                send_sem=c_send.at[way, at, i],
                recv_sem=c_recv.at[way, at, i],
                device_id={"ctx": to, "head": z},
                device_id_type=MESH,
            )
            for i, (src, dst) in enumerate(moves)
        ]

    def total_arrival(way):
        came = tot.at[way, pl.ds(other_core * half_h, half_h)]
        return pltpu.make_async_remote_copy(
            src_ref=came,
            dst_ref=came,
            send_sem=c_send.at[way, span + 1, 0],
            recv_sem=c_recv.at[way, span + 1, 0],
            device_id={"ctx": partner, "head": z},
            device_id_type=MESH,
        )

    def onward(way, k):
        return chip + k < chips if way == 0 else chip >= k

    def behind(way, k):
        return chip >= k if way == 0 else chip + k < chips

    def carry_pair(way):
        for copy in carry_copies(way, 0):
            copy.wait_recv()
        keep_near = keep(1 - way)
        early = core == way
        mine = jnp.where(early, keep_near, 1.0)
        theirs = jnp.where(early, 1.0, keep_near)

        @pl.loop(0, half_h)
        def _(i):
            h = core * half_h + i
            pair[way, i] = (mine * own[way, h].astype(f32) + theirs * oth[way, h].astype(f32)).astype(bf16)

        npair[way] = mine * nown[way] + theirs * noth[way]
        for k in range(1, span + 1):
            pl.when(onward(way, k))(lambda k=k: start_all(carry_copies(way, k)))

    def carry_arrive(way):
        for k in range(1, span + 1):

            @pl.when(behind(way, k))
            def _(k=k):
                for copy in carry_copies(way, k):
                    copy.wait_recv()

        through = [jnp.float32(1.0)]
        for k in range(2, span + 1):
            base = 2 * (k - 1) * (2 * way - 1)
            through.append(through[-1] * keep(base) * keep(base + 1))

        def weighed(stack, index):
            total = 0.0
            for k in range(1, span + 1):
                came = jnp.where(behind(way, k), stack[(way, k - 1) + index].astype(f32), 0.0)
                total = total + through[k - 1] * came
            return total

        @pl.loop(0, half_h)
        def _(i):
            tot[way, core * half_h + i] = weighed(arr, (i,)).astype(bf16)

        start_all(carry_copies(way, -1))
        near, far = carry_shares(way)
        ntot[way] = near * noth[way] + far * weighed(narr, ())

    def carry_shares(way):
        early = core == way
        return jnp.where(early, 0.0, 1.0), jnp.where(early, 1.0, keep(way))

    def carry_total(way, h):
        near, far = carry_shares(way)
        norm = jnp.broadcast_to(ntot[way, pl.ds(h, 1), :], (8, FEAT))
        return near * oth[way, h].astype(f32) + far * tot[way, h].astype(f32), norm

    carried_row = rows_ref[0, 0:1]
    ending_row = rows_ref[1, 0:1]
    ones8 = jnp.ones((8, tokens), bf16)

    def features(h):
        first, second = feature_factors(key(h))
        feat = (first * second * cols_ref[:, 2:3] * ending_row).astype(bf16)
        phik[h] = feat
        own[0, h] = (mm(feat, v_ref[:, head_rows(h)], 1, 0) * cols_ref[:, 3:4]).astype(bf16)
        nown[0, pl.ds(h, 1), :] = (mm(ones8, feat, 1, 1) * wrow_ref[...])[0:1]
        first, second = feature_factors(query(h))
        phiq[h] = (first * second * cols_ref[:, 2:3] * carried_row).astype(bf16)

    each_head(0, heads, features)
    start_all(carry_copies(0, 0))

    blocks = [(slice(0, half_t), half_t), (slice(half_t, tokens), tokens)]

    def scores_of(h, at, upto):
        return mm(key(h)[:, :upto], query(h)[:, at] * bf16(0.25), 0, 0)

    def attend(h):
        for at, upto in blocks:
            s = scores_of(h, at, upto)
            slope_ref[h, :upto, at] = (1.0 + s) * mask_ref[:upto, at]
            weight = ((0.5 * s + 1.0) * s + 1.0) * mask_ref[:upto, at]
            weight_b = weight.astype(bf16)
            wb_ref[h, :upto, at] = weight_b
            den_ref[h, :, at] = jnp.broadcast_to(
                jnp.sum(weight, axis=0, keepdims=True), (8, half_t)
            )
            y_ref[h, :, at] = mm(v_ref[:upto, head_rows(h)], weight_b, 0, 0)

    row_block = min(256, rows_all)
    blocks_of_rows = rows_all // row_block

    def upstream(n, low, high):
        if low == 0:
            for copy in w_copies(n):
                copy.wait()

        @pl.loop(0, blocks_of_rows)
        def _(b):
            at = pl.ds(pl.multiple_of(b * row_block, row_block), row_block)
            total = None if n == 0 and low == 0 else up_ref[at, :]
            for g in range(low, high):
                one = mm(wbuf[n % 2, g, at, :], out_ref[n, g], 1, 1)
                total = one if total is None else total + one
            up_ref[at, :] = total

        if high == shares and n + 2 < depth:
            start_all(w_copies(n + 2))

    each_head(0, heads // 4, attend)
    carry_pair(0)
    each_head(heads // 4, heads // 2, attend)
    arrive(1, 0)
    each_head(heads // 2, heads, attend)
    for copy in own_copies:
        copy.wait()
    upstream(0, 0, shares)
    carry_arrive(0)
    if shares > 1:
        arrive(1, 1)
    total_arrival(0).wait_recv()

    def finish_forward(h):
        state, norm = carry_total(0, h)
        state_b = state.astype(bf16)
        st_ref[h] = state_b
        feat = phiq[h]
        from_state = mm(state_b, feat, 0, 0)
        from_norm = jnp.sum(mm(split_rows(norm), feat, 1, 0), axis=0, keepdims=True)
        inverse = 1.0 / (den_ref[h, 0:1] + from_norm)
        den_ref[h] = jnp.broadcast_to(inverse, (8, tokens))
        y = (y_ref[h] + from_state) * inverse
        y_ref[h] = y
        att_ref[head_rows(h), :] = y.astype(bf16)

    each_head(0, heads, finish_forward)

    def partner_copy(m):
        return pltpu.make_async_remote_copy(
            src_ref=psend.at[m],
            dst_ref=precv.at[m],
            send_sem=p_ssem.at[m],
            recv_sem=p_rsem.at[m],
            device_id={"ctx": partner, "head": z},
            device_id_type=MESH,
        )

    def product(m):
        n, g = m // shares, m % shares

        def halves(mine):
            @pl.loop(0, blocks_of_rows)
            def _(b):
                at = pl.ds(pl.multiple_of(b * row_block, row_block), row_block)
                both_cores = mm(att_ref[at, :], out_ref[n, g], 1, 0)
                for j in range(roots):
                    to = slice(j * cg, (j + 1) * cg)
                    theirs = (2 * j + 1 - mine) * cg
                    ours = (2 * j + mine) * cg
                    psend[m, at, to] = both_cores[:, theirs : theirs + cg].astype(bf16)
                    acc[m, at, to] = both_cores[:, ours : ours + cg]

        for mine in range(2):
            pl.when(core == mine)(lambda mine=mine: halves(mine))
        partner_copy(m).start()

    if bits == 2:
        flows = [
            [({one: 1, two: 0}, two), ({one: 1, two: 1}, one), ({one: 0, two: 1}, two)]
            for one, two in ((0, 1), (1, 0))
        ]
    else:
        flows = []
        for order in (list(range(bits))[::-1], list(range(bits))):
            done = [dict.fromkeys(order[:stage], 0) for stage in range(bits)]
            flows.append([({**done[stage], b: 1}, b) for stage, b in enumerate(order)])
    stages = len(flows[0])

    def relative(m, j, b):
        root = piece(m // shares) * roots + j
        return (chip_bit[b] + (root // (1 << b)) % 2) % 2

    def matches(m, j, pattern):
        live = None
        for b, value in pattern.items():
            here = relative(m, j, b) == value
            live = here if live is None else live & here
        return live

    def sends(m, j, flow, stage):
        return matches(m, j, flows[flow][stage][0])

    def receives(m, j, flow, stage):
        pattern, b = flows[flow][stage]
        return matches(m, j, {**pattern, b: 1 - pattern[b]})

    def inbox(stage):
        return stage % rbuf.shape[1]

    def flow_rows(flow):
        return pl.ds(flow * half_r, half_r)

    def flow_columns(j):
        return pl.ds(j * cg, cg)

    def stage_copy(m, j, flow, stage):
        b = flows[flow][stage][1]
        return pltpu.make_async_remote_copy(
            src_ref=psend.at[m, flow_rows(flow), flow_columns(j)],
            dst_ref=rbuf.at[m, inbox(stage), flow_rows(flow), flow_columns(j)],
            send_sem=s_ssem.at[m, flow, j],
            recv_sem=s_rsem.at[m, inbox(stage), flow, j],
            device_id={"ctx": neighbour[b], "head": z},
            device_id_type=MESH,
        )

    def result_copy(g, flow):
        return pltpu.make_async_copy(
            pbuf.at[g, flow_rows(flow), :],
            p_out.at[flow_rows(flow), pl.ds(g * cg, cg)],
            osem.at[g, flow],
        )

    def tree(m, step):
        if step == 0:
            partner_copy(m).wait()
        for flow in range(2):
            for j in range(roots):
                at, cols = flow_rows(flow), slice(j * cg, (j + 1) * cg)
                if step == 0:
                    acc[m, at, cols] = acc[m, at, cols] + precv[m, at, cols].astype(f32)
                else:

                    @pl.when(receives(m, j, flow, step - 1))
                    def _():
                        stage_copy(m, j, flow, step - 1).wait_recv()
                        total = acc[m, at, cols] + rbuf[m, inbox(step - 1), at, cols].astype(f32)
                        if step == stages:
                            pbuf[m % shares, at, :] = total
                            result_copy(m % shares, flow).start()
                        else:
                            acc[m, at, cols] = total

                if step < stages:

                    @pl.when(sends(m, j, flow, step))
                    def _():
                        psend[m, at, cols] = acc[m, at, cols].astype(bf16)
                        stage_copy(m, j, flow, step).start()

    last = depth * shares - 1

    def trees(m):
        for step in range(stages + 1):
            if 0 <= m - LAG * step <= last:
                tree(m - LAG * step, step)

    for m in range(last):
        if m >= 2 * shares:
            arrive(m // shares, m % shares)
        if 1 < m < shares:
            arrive(1, m)
        product(m)
        n, g = m // shares, m % shares
        if n == depth - 1:
            if g == shares - 2:
                upstream(n, 0, shares - 1)
        elif n > 0 and g == shares - 1:
            upstream(n, 0, shares)
        trees(m)
    arrive(last // shares, last % shares)
    product(last)
    upstream(depth - 1, shares - 1, shares)

    def start_backward(h):
        up = up_ref[head_rows(h), :]
        inverse = den_ref[h, 0:1]
        den_grad = -jnp.sum(up * y_ref[h], axis=0, keepdims=True) * inverse
        num_grad = (up * inverse).astype(bf16)
        ng_ref[h] = num_grad
        den_rows = jnp.broadcast_to(den_grad, (8, tokens))
        dg_ref[h] = den_rows
        feat = phiq[h]
        own[1, h] = (mm(feat, num_grad, 1, 1) * cols_ref[:, 3:4]).astype(bf16)
        nadj = jnp.sum(mm(split_rows(den_rows), feat, 1, 1), axis=0, keepdims=True)
        nown[1, pl.ds(h, 1), :] = nadj * wrow_ref[0:1]

    each_head(0, heads, start_backward)
    start_all(carry_copies(1, 0))
    trees(last)
    carry_pair(1)

    def key_rows(h):
        return pl.ds(pl.multiple_of(h * 2 * QK + QK, QK), QK)

    def query_rows(h):
        return pl.ds(pl.multiple_of(h * 2 * QK, QK), QK)

    def outer(rows, dense):
        place = lax.broadcasted_iota(jnp.int32, rows.shape, 0)
        high = rows.astype(bf16).astype(f32)
        left = jnp.where(place == 2, rows - high, jnp.where(place < 2, high, 0.0)).astype(bf16)
        place = lax.broadcasted_iota(jnp.int32, dense.shape, 0)
        high = dense.astype(bf16).astype(f32)
        right = jnp.where(place == 1, dense - high, high).astype(bf16)
        return mm(left, right, 0, 0)

    def attention_grad(h):
        value_part = []
        key_part = []
        for at, upto in blocks:
            q4 = query(h)[:, at] * bf16(0.25)
            grad = ng_ref[h, :, at]
            mix = mm(v_ref[:upto, head_rows(h)], grad, 1, 0) + dg_ref[h, 0:1, at]
            score_grad = (mix * slope_ref[h, :upto, at]).astype(bf16)
            qkg[query_rows(h), at] = mm(key(h)[:, :upto] * bf16(0.25), score_grad, 1, 0)
            key_part.append(mm(score_grad, q4, 1, 1))
            value_part.append(mm(wb_ref[h, :upto, at], grad, 1, 1))
        vg_ref[h, :half_t] = value_part[0] + value_part[1][:half_t]
        vg_ref[h, half_t:] = value_part[1][half_t:]
        key_sum = jnp.concatenate([key_part[0] + key_part[1][:half_t], key_part[1][half_t:]], axis=0)
        qkg[key_rows(h), :] = key_sum.T
        grad = mm(st_ref[h], ng_ref[h], 1, 0) + outer(jnp.broadcast_to(ntot[0, pl.ds(h, 1), :], (8, FEAT)), dg_ref[h])
        first, second = feature_factors(query(h))
        qkg[query_rows(h), :] += feature_grad(grad, first, second) * carried_row

    rounds = LAG * stages
    steps = 2 * heads

    def remaining(at):
        for r in range(at * rounds // steps, (at + 1) * rounds // steps):
            trees(last + 1 + r)

    for h in range(heads):
        each_head(h, h + 1, attention_grad)
        remaining(h)
        if h == heads - 2:
            carry_arrive(1)

    total_arrival(1).wait_recv()

    def finish(h):
        adjoint, nadj = carry_total(1, h)
        adjoint_b = adjoint.astype(bf16)
        feat = phik[h]
        v_held[:, head_rows(h)] = (vg_ref[h] + mm(feat, adjoint_b, 0, 0)).astype(bf16)
        grad = mm(adjoint_b, v_ref[:, head_rows(h)], 1, 1) + mm(split_rows(nadj), ones8, 0, 0)
        first, second = feature_factors(key(h))
        qkg[key_rows(h), :] += feature_grad(grad, first, second) * ending_row

    for h in range(heads):
        each_head(h, h + 1, finish)
        remaining(heads + h)
    qk_ref[...] = qkg[...].T.astype(bf16)
    outputs = [
        pltpu.make_async_copy(qk_ref, qk_out, isem.at[0]),
        pltpu.make_async_copy(v_held, v_out, isem.at[1]),
    ]
    start_all(outputs)

    for part in range(len(parts)):
        for way in range(2):
            for k in range(depth - 1):
                pl.when(ag_cond(way, k))(
                    lambda way=way, k=k, part=part: ag(way, k, part).wait_send()
                )
    for way in range(2):
        for copy in carry_copies(way, 0) + carry_copies(way, -1):
            copy.wait_send()
        for k in range(1, span + 1):

            @pl.when(onward(way, k))
            def _(way=way, k=k):
                for copy in carry_copies(way, k):
                    copy.wait_send()

    for m in range(last + 1):
        for j in range(roots):
            for flow in range(2):
                for stage in range(stages):
                    pl.when(sends(m, j, flow, stage))(
                        lambda m=m, j=j, flow=flow, stage=stage: stage_copy(
                            m, j, flow, stage
                        ).wait_send()
                    )
    for g in range(shares):
        for flow in range(2):
            result_copy(g, flow).wait()
    for copy in outputs:
        copy.wait()


def hand_on_kernel(cuts, *refs):
    count = len(cuts)
    sources, targets, held = refs[:count], refs[count : 2 * count], refs[2 * count : 3 * count]
    sem_in, sem_out = refs[3 * count :]
    moves = []
    for n, cut in enumerate(cuts):
        size = sources[n].shape[0] // cut
        for at in range(cut):
            rows = pl.ds(at * size, size)
            place = len(moves)
            moves.append(
                (
                    pltpu.make_async_copy(sources[n].at[rows], held[n].at[rows], sem_in.at[place]),
                    pltpu.make_async_copy(held[n].at[rows], targets[n].at[rows], sem_out.at[place]),
                )
            )
    for come, _ in moves:
        come.start()
    for come, go in moves:
        come.wait()
        go.start()
    for _, go in moves:
        go.wait()


def hand_on(*arrays):
    cuts = [max(1, a.size * a.dtype.itemsize >> 18) for a in arrays]
    hbm = pl.BlockSpec(memory_space=pl.ANY)
    return pl.pallas_call(
        functools.partial(hand_on_kernel, cuts),
        name="hand_on",
        out_shape=tuple(jax.ShapeDtypeStruct(a.shape, a.dtype) for a in arrays),
        in_specs=[hbm] * len(arrays),
        out_specs=(hbm,) * len(arrays),
        scratch_shapes=[pltpu.VMEM(a.shape, a.dtype) for a in arrays]
        + [pltpu.SemaphoreType.DMA((sum(cuts),)), pltpu.SemaphoreType.DMA((sum(cuts),))],
    )(*arrays)


def on_device(query_key, values, out_grad, out_weight, doc_lengths):
    tokens = query_key.shape[0]
    rows_all = out_weight.shape[0]
    heads = rows_all // HEAD
    count = lax.axis_size("ctx")
    depth = lax.axis_size("head")
    chips = count // 2
    bits = chips.bit_length() - 1
    roots = chips // depth
    width = out_weight.shape[1] // count
    span = (DOC_MOST // tokens + 1) // 2
    shares = max(1, min(4, width // 128))
    inboxes = 1 if bits == 2 else bits
    wide = roots * width // shares
    parts = 2 * roots * shares
    pieces = depth * shares
    whole = pl.BlockSpec(memory_space=pltpu.VMEM)
    hbm = pl.BlockSpec(memory_space=pl.ANY)
    vmem = pltpu.VMEM
    dma = pltpu.SemaphoreType.DMA
    scratch = [
        vmem(query_key.shape, bf16),
        vmem(values.shape, bf16),
        vmem(values.shape, bf16),
        vmem((depth, shares, tokens, 2 * wide), bf16),
        vmem((2, shares, rows_all, 2 * wide), bf16),
        vmem((2 * QK * heads, tokens), bf16),
        vmem((2 * QK * heads, tokens), f32),
        vmem((heads, FEAT, tokens), bf16),
        vmem((heads, FEAT, tokens), bf16),
        vmem((tokens, tokens), f32),
        vmem((heads, tokens, tokens), f32),
        vmem((heads, tokens, tokens), bf16),
        vmem((heads, HEAD, tokens), f32),
        vmem((rows_all, tokens), bf16),
        vmem((rows_all, tokens), f32),
        vmem((heads, HEAD, tokens), bf16),
        vmem((heads, 8, tokens), f32),
        vmem((heads, 8, tokens), f32),
        vmem((2, 8, tokens), f32),
        vmem((heads, FEAT, HEAD), bf16),
        vmem((2, heads, FEAT, HEAD), bf16),
        vmem((2, heads, FEAT, HEAD), bf16),
        vmem((2, heads // 2, FEAT, HEAD), bf16),
        vmem((2, span, heads // 2, FEAT, HEAD), bf16),
        vmem((2, heads, FEAT, HEAD), bf16),
        vmem((2, heads, FEAT), f32),
        vmem((2, heads, FEAT), f32),
        vmem((2, heads, FEAT), f32),
        vmem((2, span, heads, FEAT), f32),
        vmem((2, heads, FEAT), f32),
        vmem((heads, tokens, HEAD), f32),
        vmem((pieces, rows_all, wide), f32),
        vmem((pieces, rows_all, wide), bf16),
        vmem((pieces, rows_all, wide), bf16),
        vmem((pieces, inboxes, rows_all, wide), bf16),
        vmem((shares, rows_all, width // shares), f32),
        dma((2,)),
        dma((2, parts)),
        dma((parts,)),
        dma((shares, 2)),
        dma((2, depth, parts)),
        dma((2, depth, parts)),
        dma((2, span + 2, 2)),
        dma((2, span + 2, 2)),
        dma((pieces,)),
        dma((pieces,)),
        dma((pieces, 2, roots)),
        dma((pieces, inboxes, 2, roots)),
    ]
    results = pl.pallas_call(
        functools.partial(kernel, count, depth),
        name="step",
        out_shape=(
            jax.ShapeDtypeStruct(query_key.shape, bf16),
            jax.ShapeDtypeStruct(values.shape, bf16),
            jax.ShapeDtypeStruct((rows_all, width), f32),
        ),
        in_specs=[
            pl.BlockSpec(memory_space=pltpu.SMEM),
            hbm,
            hbm,
            hbm,
            hbm,
            whole,
            whole,
            whole,
            whole,
            whole,
            whole,
        ],
        out_specs=(hbm, hbm, hbm),
        scratch_shapes=scratch,
        compiler_params=pltpu.CompilerParams(
            collective_id=0, has_side_effects=True, vmem_limit_bytes=67_043_328
        ),
    )(
        doc_lengths,
        query_key,
        values,
        out_grad,
        out_weight,
        jnp.asarray(LEFT, bf16),
        jnp.asarray(RIGHT, bf16),
        jnp.asarray(LEFT.T, bf16),
        jnp.asarray(RIGHT.T, bf16),
        jnp.asarray(COLS),
        jnp.asarray(np.broadcast_to(COLS[:, 3][None], (8, FEAT)).copy()),
    )
    return hand_on(*results)


def solution(mesh):
    placed = (P("ctx", "head"), P("ctx", "head"), P("ctx", "head"), P("head", None), P())
    return jax.shard_map(
        on_device,
        mesh=mesh,
        in_specs=placed,
        out_specs=(P("ctx", "head"), P("ctx", "head"), P("head", "ctx")),
        check_vma=False,
    )
```

```python
import functools
import math

import jax
import jax.numpy as jnp
import numpy as np
from jax import lax
from jax.experimental import pallas as pl
from jax.experimental.pallas import tpu as pltpu
from jax.sharding import PartitionSpec as P

HEAD = 128
QK = 16
DOC_MOST = 2048
LAG = 2

quad_scale = 0.25 / math.sqrt(2.0)

bf16 = jnp.bfloat16
f32 = jnp.float32
MESH = pl.DeviceIdType.MESH

PAIRS = [(a, b) for a in range(QK) for b in range(a, QK)]
FEAT = 160


def tables():
    left = np.zeros((FEAT, QK), np.float32)
    right = np.zeros((FEAT, QK), np.float32)
    cols = np.zeros((FEAT, 4), np.float32)
    cols[0, 0] = cols[0, 1] = cols[0, 2] = 1.0
    cols[:, 3] = 1.0
    for a in range(QK):
        left[1 + a, a] = 1.0
        cols[1 + a, 1] = 1.0
        cols[1 + a, 2] = 0.5
    for place, (a, b) in enumerate(PAIRS):
        left[1 + QK + place, a] = 1.0
        right[1 + QK + place, b] = 1.0
        cols[1 + QK + place, 2] = quad_scale
        cols[1 + QK + place, 3] = 1.0 if a == b else 2.0
    return left, right, cols


LEFT, RIGHT, COLS = tables()


def mm(a, b, ca, cb):
    return lax.dot_general(a, b, (((ca,), (cb,)), ((), ())), preferred_element_type=f32)


def split_rows(rows):
    high = rows.astype(bf16).astype(f32)
    place = lax.broadcasted_iota(jnp.int32, rows.shape, 0)
    return jnp.where(place == 0, high, jnp.where(place == 1, rows - high, 0.0)).astype(bf16)


def kernel(
    count,
    depth,
    docs_ref,
    qk_hbm,
    v_hbm,
    g_ref,
    w_ref,
    lcol_ref,
    rcol_ref,
    lrow_ref,
    rrow_ref,
    cols_ref,
    wrow_ref,
    qk_out,
    v_out,
    p_out,
    qk_ref,
    v_ref,
    v_held,
    out_ref,
    wbuf,
    qkt,
    qkg,
    phiq,
    phik,
    mask_ref,
    slope_ref,
    wb_ref,
    y_ref,
    att_ref,
    up_ref,
    ng_ref,
    den_ref,
    dg_ref,
    rows_ref,
    st_ref,
    own,
    oth,
    pair,
    arr,
    tot,
    nown,
    noth,
    npair,
    narr,
    ntot,
    vg_ref,
    acc,
    psend,
    precv,
    rbuf,
    pbuf,
    isem,
    wsem,
    gsem,
    osem,
    ag_send,
    ag_recv,
    c_send,
    c_recv,
    p_ssem,
    p_rsem,
    s_ssem,
    s_rsem,
):
    tokens = qk_hbm.shape[0]
    heads = v_hbm.shape[1] // HEAD
    rows_all = heads * HEAD
    shard = g_ref.shape[1]
    chips = count // 2
    bits = chips.bit_length() - 1
    roots = chips // depth
    cw = shard // (2 * roots)
    half_t = tokens // 2
    half_h = heads // 2
    shares = acc.shape[0] // depth
    cg = cw // shares
    half_r = rows_all // 2
    span = arr.shape[1]
    c = lax.axis_index("ctx")
    z = lax.axis_index("head")
    chip = c // 2
    core = c % 2
    other_core = 1 - core
    partner = 2 * chip + other_core
    chip_bit = [(chip // (1 << b)) % 2 for b in range(bits)]
    neighbour = [2 * (chip + (1 - 2 * chip_bit[b]) * (1 << b)) + core for b in range(bits)]

    barrier = pltpu.get_barrier_semaphore()

    met = [(None, {"ctx": partner, "head": z})]
    met += [(z > 0, {"ctx": c, "head": z - 1}), (z < depth - 1, {"ctx": c, "head": z + 1})]
    met += [(None, {"ctx": neighbour[b], "head": z}) for b in range(bits) if (1 << b) > span]
    for k in range(1, span + 1):
        met += [
            (chip >= k, {"ctx": c - 2 * k, "head": z}),
            (chip + k < chips, {"ctx": c + 2 * k, "head": z}),
        ]
    peers = 0
    for cond, where in met:

        def greet(where=where):
            pl.semaphore_signal(barrier, inc=1, device_id=where, device_id_type=MESH)

        if cond is None:
            greet()
            peers = peers + 1
        else:
            pl.when(cond)(greet)
            peers = peers + cond.astype(jnp.int32)
    pl.semaphore_wait(barrier, peers)

    def piece(n):
        if n == 0:
            return z
        k = (n + 1) // 2
        inner = z - k if n % 2 else z + k
        low_side = 1 - (2 * z + 1) // depth
        lesser = low_side * z + (1 - low_side) * (depth - 1 - z)
        outer = low_side * n + (1 - low_side) * (depth - 1 - n)
        beyond = (n - 2 * lesser - 1 + 4 * depth) // (4 * depth)
        return (1 - beyond) * inner + beyond * outer

    def slot(way, k, level):
        if k == 0:
            return 0
        low_side = 1 - (2 * level + 1) // depth
        lesser = low_side * level + (1 - low_side) * (depth - 1 - level)
        beyond = (k - lesser - 1 + 2 * depth) // (2 * depth)
        return (1 - beyond) * (2 * k - 1 + way) + beyond * (lesser + k)

    parts = [(g, j, which) for g in range(shares) for j in range(roots) for which in range(2)]

    def part_slice(part):
        g, j, which = parts[part]
        return pl.ds((2 * j + which) * cw + g * cg, cg)

    def held_at(place, part):
        g, j, which = parts[part]
        return out_ref.at[place, g, :, pl.ds((2 * j + which) * cg, cg)]

    def ag(way, k, part):
        to = z + 1 - 2 * way
        if k == 0:
            src = g_ref.at[:, part_slice(part)]
        else:
            src = held_at(slot(way, k, z), part)
        return pltpu.make_async_remote_copy(
            src_ref=src,
            dst_ref=held_at(slot(way, k + 1, to), part),
            send_sem=ag_send.at[way, k, part],
            recv_sem=ag_recv.at[way, k, part],
            device_id={"ctx": c, "head": to},
            device_id_type=MESH,
        )

    def ag_arrival(way, k, part):
        came = held_at(slot(way, k, z), part)
        return pltpu.make_async_remote_copy(
            src_ref=came,
            dst_ref=came,
            send_sem=ag_send.at[way, k, part],
            recv_sem=ag_recv.at[way, k - 1, part],
            device_id={"ctx": c, "head": z - 1 + 2 * way},
            device_id_type=MESH,
        )

    def ag_cond(way, k):
        if way == 0:
            return (z >= k) & (z < depth - 1)
        return (z + k <= depth - 1) & (z > 0)

    def ag_has(way, k):
        return z >= k if way == 0 else z + k <= depth - 1

    for part in range(len(parts)):
        for way in range(2):
            pl.when(ag_cond(way, 0))(lambda way=way, part=part: ag(way, 0, part).start())

    def arrive(k, share):
        for part in range(len(parts)):
            for way in range(2):
                if parts[part][0] == share:

                    @pl.when(ag_has(way, k))
                    def _(way=way, part=part):
                        ag_arrival(way, k, part).wait_recv()

                    if k < depth - 1:
                        pl.when(ag_cond(way, k))(
                            lambda way=way, part=part: ag(way, k, part).start()
                        )

    own_copies = [
        pltpu.make_async_copy(g_ref.at[:, part_slice(part)], held_at(0, part), gsem.at[part])
        for part in range(len(parts))
    ]
    for copy in own_copies:
        copy.start()

    def w_copies(n):
        at = piece(n) * shard
        copies = []
        for part, (g, j, which) in enumerate(parts):
            start = pl.multiple_of(at + ((2 * j + which) * cw + g * cg), cg)
            copies.append(
                pltpu.make_async_copy(
                    w_ref.at[:, pl.ds(start, cg)],
                    wbuf.at[n % 2, g, :, pl.ds((2 * j + which) * cg, cg)],
                    wsem.at[n % 2, part],
                )
            )
        return copies

    def start_all(copies):
        for copy in copies:
            copy.start()

    for n in range(min(2, depth)):
        start_all(w_copies(n))

    inputs = [
        pltpu.make_async_copy(qk_hbm, qk_ref, isem.at[0]),
        pltpu.make_async_copy(v_hbm, v_ref, isem.at[1]),
    ]
    start_all(inputs)

    places_row = c * tokens + lax.broadcasted_iota(jnp.int32, (1, tokens), 1)
    places_col = c * tokens + lax.broadcasted_iota(jnp.int32, (tokens, 1), 0)
    low_edge, edge_count = -2 * (span - 1), 4 * span - 1
    bounds = [(2 * chip + low_edge + e) * tokens - 1 for e in range(edge_count)]

    def doc(d, carry):
        start, row, col, counts = carry
        row = row + (start <= places_row).astype(jnp.int32)
        col = col + (start <= places_col).astype(jnp.int32)
        counts = tuple(
            n + jnp.where(start <= bound, 1, 0) for n, bound in zip(counts, bounds)
        )
        return start + docs_ref[d], row, col, counts

    _, seg_row, seg_col, counts = lax.fori_loop(
        0,
        docs_ref.shape[0],
        doc,
        (
            jnp.int32(0),
            jnp.zeros((1, tokens), jnp.int32),
            jnp.zeros((tokens, 1), jnp.int32),
            tuple(jnp.int32(0) for _ in range(edge_count)),
        ),
    )

    def edges(offset):
        return counts[offset - low_edge]

    def keep(offset):
        block = 2 * chip + offset
        inside = (block >= 0) & (block < count)
        return jnp.where(inside, jnp.where(edges(offset) == edges(offset + 1), 1.0, 0.0), 0.0)

    before = jnp.where(core == 0, edges(0), edges(1))
    after = jnp.where(core == 0, edges(1), edges(2))
    rows_ref[0] = jnp.broadcast_to((seg_row == before).astype(f32), (8, tokens))
    rows_ref[1] = jnp.broadcast_to((seg_row == after).astype(f32), (8, tokens))
    for r in range(tokens // 128):
        at = slice(r * 128, (r + 1) * 128)
        jj = r * 128 + lax.broadcasted_iota(jnp.int32, (128, tokens), 0)
        ii = lax.broadcasted_iota(jnp.int32, (128, tokens), 1)
        same = seg_col[at] == seg_row
        mask_ref[at, :] = jnp.where(jj <= ii, jnp.where(same, 1.0, 0.0), 0.0)

    for copy in inputs:
        copy.wait()
    qkt[...] = qk_ref[...].astype(f32).T.astype(bf16)

    def head_rows(h):
        return pl.ds(pl.multiple_of(h * HEAD, HEAD), HEAD)

    def query(h):
        return qkt[pl.ds(pl.multiple_of(h * 2 * QK, QK), QK), :]

    def key(h):
        return qkt[pl.ds(pl.multiple_of(h * 2 * QK + QK, QK), QK), :]

    def feature_factors(points):
        first = mm(lcol_ref[...], points, 1, 0) + cols_ref[:, 0:1]
        second = mm(rcol_ref[...], points, 1, 0) + cols_ref[:, 1:2]
        return first, second

    def feature_grad(grad, first, second):
        scaled = grad * cols_ref[:, 2:3]
        return mm(lrow_ref[...], (scaled * second).astype(bf16), 1, 0) + mm(
            rrow_ref[...], (scaled * first).astype(bf16), 1, 0
        )

    def each_head(first, last, body):
        @pl.loop(first, last)
        def _(h):
            body(h)

    def my_heads():
        return pl.ds(core * half_h, half_h)

    def carry_copies(way, k):
        to = c + 2 * k * (1 - 2 * way) if k > 0 else partner
        if k == 0:
            moves = [(own.at[way], oth.at[way]), (nown.at[way], noth.at[way])]
        elif k > 0:
            moves = [(pair.at[way], arr.at[way, k - 1]), (npair.at[way], narr.at[way, k - 1])]
        else:
            moves = [(tot.at[way, my_heads()], tot.at[way, my_heads()])]
        at = k if k >= 0 else span + 1
        return [
            pltpu.make_async_remote_copy(
                src_ref=src,
                dst_ref=dst,
                send_sem=c_send.at[way, at, i],
                recv_sem=c_recv.at[way, at, i],
                device_id={"ctx": to, "head": z},
                device_id_type=MESH,
            )
            for i, (src, dst) in enumerate(moves)
        ]

    def total_arrival(way):
        came = tot.at[way, pl.ds(other_core * half_h, half_h)]
        return pltpu.make_async_remote_copy(
            src_ref=came,
            dst_ref=came,
            send_sem=c_send.at[way, span + 1, 0],
            recv_sem=c_recv.at[way, span + 1, 0],
            device_id={"ctx": partner, "head": z},
            device_id_type=MESH,
        )

    def onward(way, k):
        return chip + k < chips if way == 0 else chip >= k

    def behind(way, k):
        return chip >= k if way == 0 else chip + k < chips

    def carry_pair(way):
        for copy in carry_copies(way, 0):
            copy.wait_recv()
        keep_near = keep(1 - way)
        early = core == way
        mine = jnp.where(early, keep_near, 1.0)
        theirs = jnp.where(early, 1.0, keep_near)

        @pl.loop(0, half_h)
        def _(i):
            h = core * half_h + i
            pair[way, i] = (mine * own[way, h].astype(f32) + theirs * oth[way, h].astype(f32)).astype(bf16)

        npair[way] = mine * nown[way] + theirs * noth[way]
        for k in range(1, span + 1):
            pl.when(onward(way, k))(lambda k=k: start_all(carry_copies(way, k)))

    def carry_arrive(way):
        for k in range(1, span + 1):

            @pl.when(behind(way, k))
            def _(k=k):
                for copy in carry_copies(way, k):
                    copy.wait_recv()

        through = [jnp.float32(1.0)]
        for k in range(2, span + 1):
            base = 2 * (k - 1) * (2 * way - 1)
            through.append(through[-1] * keep(base) * keep(base + 1))

        def weighed(stack, index):
            total = 0.0
            for k in range(1, span + 1):
                came = jnp.where(behind(way, k), stack[(way, k - 1) + index].astype(f32), 0.0)
                total = total + through[k - 1] * came
            return total

        @pl.loop(0, half_h)
        def _(i):
            tot[way, core * half_h + i] = weighed(arr, (i,)).astype(bf16)

        start_all(carry_copies(way, -1))
        near, far = carry_shares(way)
        ntot[way] = near * noth[way] + far * weighed(narr, ())

    def carry_shares(way):
        early = core == way
        return jnp.where(early, 0.0, 1.0), jnp.where(early, 1.0, keep(way))

    def carry_total(way, h):
        near, far = carry_shares(way)
        norm = jnp.broadcast_to(ntot[way, pl.ds(h, 1), :], (8, FEAT))
        return near * oth[way, h].astype(f32) + far * tot[way, h].astype(f32), norm

    carried_row = rows_ref[0, 0:1]
    ending_row = rows_ref[1, 0:1]
    ones8 = jnp.ones((8, tokens), bf16)

    def features(h):
        first, second = feature_factors(key(h))
        feat = (first * second * cols_ref[:, 2:3] * ending_row).astype(bf16)
        phik[h] = feat
        own[0, h] = (mm(feat, v_ref[:, head_rows(h)], 1, 0) * cols_ref[:, 3:4]).astype(bf16)
        nown[0, pl.ds(h, 1), :] = (mm(ones8, feat, 1, 1) * wrow_ref[...])[0:1]
        first, second = feature_factors(query(h))
        phiq[h] = (first * second * cols_ref[:, 2:3] * carried_row).astype(bf16)

    each_head(0, heads, features)
    start_all(carry_copies(0, 0))

    blocks = [(slice(0, half_t), half_t), (slice(half_t, tokens), tokens)]

    def scores_of(h, at, upto):
        return mm(key(h)[:, :upto], query(h)[:, at] * bf16(0.25), 0, 0)

    def attend(h):
        for at, upto in blocks:
            s = scores_of(h, at, upto)
            slope_ref[h, :upto, at] = (1.0 + s) * mask_ref[:upto, at]
            weight = ((0.5 * s + 1.0) * s + 1.0) * mask_ref[:upto, at]
            weight_b = weight.astype(bf16)
            wb_ref[h, :upto, at] = weight_b
            den_ref[h, :, at] = jnp.broadcast_to(
                jnp.sum(weight, axis=0, keepdims=True), (8, half_t)
            )
            y_ref[h, :, at] = mm(v_ref[:upto, head_rows(h)], weight_b, 0, 0)

    row_block = min(256, rows_all)
    blocks_of_rows = rows_all // row_block

    def upstream(n, low, high):
        if low == 0:
            for copy in w_copies(n):
                copy.wait()

        @pl.loop(0, blocks_of_rows)
        def _(b):
            at = pl.ds(pl.multiple_of(b * row_block, row_block), row_block)
            total = None if n == 0 and low == 0 else up_ref[at, :]
            for g in range(low, high):
                one = mm(wbuf[n % 2, g, at, :], out_ref[n, g], 1, 1)
                total = one if total is None else total + one
            up_ref[at, :] = total

        if high == shares and n + 2 < depth:
            start_all(w_copies(n + 2))

    each_head(0, heads // 4, attend)
    carry_pair(0)
    each_head(heads // 4, heads // 2, attend)
    arrive(1, 0)
    each_head(heads // 2, heads, attend)
    for copy in own_copies:
        copy.wait()
    upstream(0, 0, shares)
    carry_arrive(0)
    if shares > 1:
        arrive(1, 1)
    total_arrival(0).wait_recv()

    def finish_forward(h):
        state, norm = carry_total(0, h)
        state_b = state.astype(bf16)
        st_ref[h] = state_b
        feat = phiq[h]
        from_state = mm(state_b, feat, 0, 0)
        from_norm = jnp.sum(mm(split_rows(norm), feat, 1, 0), axis=0, keepdims=True)
        inverse = 1.0 / (den_ref[h, 0:1] + from_norm)
        den_ref[h] = jnp.broadcast_to(inverse, (8, tokens))
        y = (y_ref[h] + from_state) * inverse
        y_ref[h] = y
        att_ref[head_rows(h), :] = y.astype(bf16)

    each_head(0, heads, finish_forward)

    def partner_copy(m):
        return pltpu.make_async_remote_copy(
            src_ref=psend.at[m],
            dst_ref=precv.at[m],
            send_sem=p_ssem.at[m],
            recv_sem=p_rsem.at[m],
            device_id={"ctx": partner, "head": z},
            device_id_type=MESH,
        )

    def product(m):
        n, g = m // shares, m % shares

        def halves(mine):
            @pl.loop(0, blocks_of_rows)
            def _(b):
                at = pl.ds(pl.multiple_of(b * row_block, row_block), row_block)
                both_cores = mm(att_ref[at, :], out_ref[n, g], 1, 0)
                for j in range(roots):
                    to = slice(j * cg, (j + 1) * cg)
                    theirs = (2 * j + 1 - mine) * cg
                    ours = (2 * j + mine) * cg
                    psend[m, at, to] = both_cores[:, theirs : theirs + cg].astype(bf16)
                    acc[m, at, to] = both_cores[:, ours : ours + cg]

        for mine in range(2):
            pl.when(core == mine)(lambda mine=mine: halves(mine))
        partner_copy(m).start()

    if bits == 2:
        flows = [
            [({one: 1, two: 0}, two), ({one: 1, two: 1}, one), ({one: 0, two: 1}, two)]
            for one, two in ((0, 1), (1, 0))
        ]
    else:
        flows = []
        for order in (list(range(bits))[::-1], list(range(bits))):
            done = [dict.fromkeys(order[:stage], 0) for stage in range(bits)]
            flows.append([({**done[stage], b: 1}, b) for stage, b in enumerate(order)])
    stages = len(flows[0])

    def relative(m, j, b):
        root = piece(m // shares) * roots + j
        return (chip_bit[b] + (root // (1 << b)) % 2) % 2

    def matches(m, j, pattern):
        live = None
        for b, value in pattern.items():
            here = relative(m, j, b) == value
            live = here if live is None else live & here
        return live

    def sends(m, j, flow, stage):
        return matches(m, j, flows[flow][stage][0])

    def receives(m, j, flow, stage):
        pattern, b = flows[flow][stage]
        return matches(m, j, {**pattern, b: 1 - pattern[b]})

    def inbox(stage):
        return stage % rbuf.shape[1]

    def flow_rows(flow):
        return pl.ds(flow * half_r, half_r)

    def flow_columns(j):
        return pl.ds(j * cg, cg)

    def stage_copy(m, j, flow, stage):
        b = flows[flow][stage][1]
        return pltpu.make_async_remote_copy(
            src_ref=psend.at[m, flow_rows(flow), flow_columns(j)],
            dst_ref=rbuf.at[m, inbox(stage), flow_rows(flow), flow_columns(j)],
            send_sem=s_ssem.at[m, flow, j],
            recv_sem=s_rsem.at[m, inbox(stage), flow, j],
            device_id={"ctx": neighbour[b], "head": z},
            device_id_type=MESH,
        )

    def result_copy(g, flow):
        return pltpu.make_async_copy(
            pbuf.at[g, flow_rows(flow), :],
            p_out.at[flow_rows(flow), pl.ds(g * cg, cg)],
            osem.at[g, flow],
        )

    def tree(m, step):
        if step == 0:
            partner_copy(m).wait()
        for flow in range(2):
            for j in range(roots):
                at, cols = flow_rows(flow), slice(j * cg, (j + 1) * cg)
                if step == 0:
                    acc[m, at, cols] = acc[m, at, cols] + precv[m, at, cols].astype(f32)
                else:

                    @pl.when(receives(m, j, flow, step - 1))
                    def _():
                        stage_copy(m, j, flow, step - 1).wait_recv()
                        total = acc[m, at, cols] + rbuf[m, inbox(step - 1), at, cols].astype(f32)
                        if step == stages:
                            pbuf[m % shares, at, :] = total
                            result_copy(m % shares, flow).start()
                        else:
                            acc[m, at, cols] = total

                if step < stages:

                    @pl.when(sends(m, j, flow, step))
                    def _():
                        psend[m, at, cols] = acc[m, at, cols].astype(bf16)
                        stage_copy(m, j, flow, step).start()

    last = depth * shares - 1

    def trees(m):
        for step in range(stages + 1):
            if 0 <= m - LAG * step <= last:
                tree(m - LAG * step, step)

    for m in range(last):
        if m >= 2 * shares:
            arrive(m // shares, m % shares)
        if 1 < m < shares:
            arrive(1, m)
        product(m)
        n, g = m // shares, m % shares
        if n == depth - 1:
            if g == shares - 2:
                upstream(n, 0, shares - 1)
        elif n > 0 and g == shares - 1:
            upstream(n, 0, shares)
        trees(m)
    arrive(last // shares, last % shares)
    product(last)
    upstream(depth - 1, shares - 1, shares)

    def start_backward(h):
        up = up_ref[head_rows(h), :]
        inverse = den_ref[h, 0:1]
        den_grad = -jnp.sum(up * y_ref[h], axis=0, keepdims=True) * inverse
        num_grad = (up * inverse).astype(bf16)
        ng_ref[h] = num_grad
        den_rows = jnp.broadcast_to(den_grad, (8, tokens))
        dg_ref[h] = den_rows
        feat = phiq[h]
        own[1, h] = (mm(feat, num_grad, 1, 1) * cols_ref[:, 3:4]).astype(bf16)
        nadj = jnp.sum(mm(split_rows(den_rows), feat, 1, 1), axis=0, keepdims=True)
        nown[1, pl.ds(h, 1), :] = nadj * wrow_ref[0:1]

    each_head(0, heads, start_backward)
    start_all(carry_copies(1, 0))
    trees(last)
    carry_pair(1)

    def key_rows(h):
        return pl.ds(pl.multiple_of(h * 2 * QK + QK, QK), QK)

    def query_rows(h):
        return pl.ds(pl.multiple_of(h * 2 * QK, QK), QK)

    def outer(rows, dense):
        place = lax.broadcasted_iota(jnp.int32, rows.shape, 0)
        high = rows.astype(bf16).astype(f32)
        left = jnp.where(place == 2, rows - high, jnp.where(place < 2, high, 0.0)).astype(bf16)
        place = lax.broadcasted_iota(jnp.int32, dense.shape, 0)
        high = dense.astype(bf16).astype(f32)
        right = jnp.where(place == 1, dense - high, high).astype(bf16)
        return mm(left, right, 0, 0)

    def attention_grad(h):
        value_part = []
        key_part = []
        for at, upto in blocks:
            q4 = query(h)[:, at] * bf16(0.25)
            grad = ng_ref[h, :, at]
            mix = mm(v_ref[:upto, head_rows(h)], grad, 1, 0) + dg_ref[h, 0:1, at]
            score_grad = (mix * slope_ref[h, :upto, at]).astype(bf16)
            qkg[query_rows(h), at] = mm(key(h)[:, :upto] * bf16(0.25), score_grad, 1, 0)
            key_part.append(mm(score_grad, q4, 1, 1))
            value_part.append(mm(wb_ref[h, :upto, at], grad, 1, 1))
        vg_ref[h, :half_t] = value_part[0] + value_part[1][:half_t]
        vg_ref[h, half_t:] = value_part[1][half_t:]
        key_sum = jnp.concatenate([key_part[0] + key_part[1][:half_t], key_part[1][half_t:]], axis=0)
        qkg[key_rows(h), :] = key_sum.T
        grad = mm(st_ref[h], ng_ref[h], 1, 0) + outer(jnp.broadcast_to(ntot[0, pl.ds(h, 1), :], (8, FEAT)), dg_ref[h])
        first, second = feature_factors(query(h))
        qkg[query_rows(h), :] += feature_grad(grad, first, second) * carried_row

    rounds = LAG * stages
    steps = heads + 2

    def remaining(at):
        for r in range(at * rounds // steps, (at + 1) * rounds // steps):
            trees(last + 1 + r)

    for h in range(heads):
        each_head(h, h + 1, attention_grad)
        remaining(h)
        if h == heads - 1:
            carry_arrive(1)

    total_arrival(1).wait_recv()

    def finish(h):
        adjoint, nadj = carry_total(1, h)
        adjoint_b = adjoint.astype(bf16)
        feat = phik[h]
        v_held[:, head_rows(h)] = (vg_ref[h] + mm(feat, adjoint_b, 0, 0)).astype(bf16)
        grad = mm(adjoint_b, v_ref[:, head_rows(h)], 1, 1) + mm(split_rows(nadj), ones8, 0, 0)
        first, second = feature_factors(key(h))
        qkg[key_rows(h), :] += feature_grad(grad, first, second) * ending_row

    for h in range(heads):
        each_head(h, h + 1, finish)
        remaining(heads + h)
    qk_ref[...] = qkg[...].T.astype(bf16)
    outputs = [
        pltpu.make_async_copy(qk_ref, qk_out, isem.at[0]),
        pltpu.make_async_copy(v_held, v_out, isem.at[1]),
    ]
    start_all(outputs)

    for part in range(len(parts)):
        for way in range(2):
            for k in range(depth - 1):
                pl.when(ag_cond(way, k))(
                    lambda way=way, k=k, part=part: ag(way, k, part).wait_send()
                )
    for way in range(2):
        for copy in carry_copies(way, 0) + carry_copies(way, -1):
            copy.wait_send()
        for k in range(1, span + 1):

            @pl.when(onward(way, k))
            def _(way=way, k=k):
                for copy in carry_copies(way, k):
                    copy.wait_send()

    for m in range(last + 1):
        for j in range(roots):
            for flow in range(2):
                for stage in range(stages):
                    pl.when(sends(m, j, flow, stage))(
                        lambda m=m, j=j, flow=flow, stage=stage: stage_copy(
                            m, j, flow, stage
                        ).wait_send()
                    )
    for g in range(shares):
        for flow in range(2):
            result_copy(g, flow).wait()
    for copy in outputs:
        copy.wait()


def hand_on_kernel(cuts, *refs):
    count = len(cuts)
    sources, targets, held = refs[:count], refs[count : 2 * count], refs[2 * count : 3 * count]
    sem_in, sem_out = refs[3 * count :]
    moves = []
    for n, cut in enumerate(cuts):
        size = sources[n].shape[0] // cut
        for at in range(cut):
            rows = pl.ds(at * size, size)
            place = len(moves)
            moves.append(
                (
                    pltpu.make_async_copy(sources[n].at[rows], held[n].at[rows], sem_in.at[place]),
                    pltpu.make_async_copy(held[n].at[rows], targets[n].at[rows], sem_out.at[place]),
                )
            )
    for come, _ in moves:
        come.start()
    for come, go in moves:
        come.wait()
        go.start()
    for _, go in moves:
        go.wait()


def hand_on(*arrays):
    cuts = [max(1, a.size * a.dtype.itemsize >> 18) for a in arrays]
    hbm = pl.BlockSpec(memory_space=pl.ANY)
    return pl.pallas_call(
        functools.partial(hand_on_kernel, cuts),
        name="hand_on",
        out_shape=tuple(jax.ShapeDtypeStruct(a.shape, a.dtype) for a in arrays),
        in_specs=[hbm] * len(arrays),
        out_specs=(hbm,) * len(arrays),
        scratch_shapes=[pltpu.VMEM(a.shape, a.dtype) for a in arrays]
        + [pltpu.SemaphoreType.DMA((sum(cuts),)), pltpu.SemaphoreType.DMA((sum(cuts),))],
    )(*arrays)


def on_device(query_key, values, out_grad, out_weight, doc_lengths):
    tokens = query_key.shape[0]
    rows_all = out_weight.shape[0]
    heads = rows_all // HEAD
    count = lax.axis_size("ctx")
    depth = lax.axis_size("head")
    chips = count // 2
    bits = chips.bit_length() - 1
    roots = chips // depth
    width = out_weight.shape[1] // count
    span = (DOC_MOST // tokens + 1) // 2
    shares = max(1, min(4, width // 128))
    inboxes = 1 if bits == 2 else bits
    wide = roots * width // shares
    parts = 2 * roots * shares
    pieces = depth * shares
    whole = pl.BlockSpec(memory_space=pltpu.VMEM)
    hbm = pl.BlockSpec(memory_space=pl.ANY)
    vmem = pltpu.VMEM
    dma = pltpu.SemaphoreType.DMA
    scratch = [
        vmem(query_key.shape, bf16),
        vmem(values.shape, bf16),
        vmem(values.shape, bf16),
        vmem((depth, shares, tokens, 2 * wide), bf16),
        vmem((2, shares, rows_all, 2 * wide), bf16),
        vmem((2 * QK * heads, tokens), bf16),
        vmem((2 * QK * heads, tokens), f32),
        vmem((heads, FEAT, tokens), bf16),
        vmem((heads, FEAT, tokens), bf16),
        vmem((tokens, tokens), f32),
        vmem((heads, tokens, tokens), f32),
        vmem((heads, tokens, tokens), bf16),
        vmem((heads, HEAD, tokens), f32),
        vmem((rows_all, tokens), bf16),
        vmem((rows_all, tokens), f32),
        vmem((heads, HEAD, tokens), bf16),
        vmem((heads, 8, tokens), f32),
        vmem((heads, 8, tokens), f32),
        vmem((2, 8, tokens), f32),
        vmem((heads, FEAT, HEAD), bf16),
        vmem((2, heads, FEAT, HEAD), bf16),
        vmem((2, heads, FEAT, HEAD), bf16),
        vmem((2, heads // 2, FEAT, HEAD), bf16),
        vmem((2, span, heads // 2, FEAT, HEAD), bf16),
        vmem((2, heads, FEAT, HEAD), bf16),
        vmem((2, heads, FEAT), f32),
        vmem((2, heads, FEAT), f32),
        vmem((2, heads, FEAT), f32),
        vmem((2, span, heads, FEAT), f32),
        vmem((2, heads, FEAT), f32),
        vmem((heads, tokens, HEAD), f32),
        vmem((pieces, rows_all, wide), f32),
        vmem((pieces, rows_all, wide), bf16),
        vmem((pieces, rows_all, wide), bf16),
        vmem((pieces, inboxes, rows_all, wide), bf16),
        vmem((shares, rows_all, width // shares), f32),
        dma((2,)),
        dma((2, parts)),
        dma((parts,)),
        dma((shares, 2)),
        dma((2, depth, parts)),
        dma((2, depth, parts)),
        dma((2, span + 2, 2)),
        dma((2, span + 2, 2)),
        dma((pieces,)),
        dma((pieces,)),
        dma((pieces, 2, roots)),
        dma((pieces, inboxes, 2, roots)),
    ]
    results = pl.pallas_call(
        functools.partial(kernel, count, depth),
        name="step",
        out_shape=(
            jax.ShapeDtypeStruct(query_key.shape, bf16),
            jax.ShapeDtypeStruct(values.shape, bf16),
            jax.ShapeDtypeStruct((rows_all, width), f32),
        ),
        in_specs=[
            pl.BlockSpec(memory_space=pltpu.SMEM),
            hbm,
            hbm,
            hbm,
            hbm,
            whole,
            whole,
            whole,
            whole,
            whole,
            whole,
        ],
        out_specs=(hbm, hbm, hbm),
        scratch_shapes=scratch,
        compiler_params=pltpu.CompilerParams(
            collective_id=0, has_side_effects=True, vmem_limit_bytes=67_043_328
        ),
    )(
        doc_lengths,
        query_key,
        values,
        out_grad,
        out_weight,
        jnp.asarray(LEFT, bf16),
        jnp.asarray(RIGHT, bf16),
        jnp.asarray(LEFT.T, bf16),
        jnp.asarray(RIGHT.T, bf16),
        jnp.asarray(COLS),
        jnp.asarray(np.broadcast_to(COLS[:, 3][None], (8, FEAT)).copy()),
    )
    return hand_on(*results)


def solution(mesh):
    placed = (P("ctx", "head"), P("ctx", "head"), P("ctx", "head"), P("head", None), P())
    return jax.shard_map(
        on_device,
        mesh=mesh,
        in_specs=placed,
        out_specs=(P("ctx", "head"), P("ctx", "head"), P("head", "ctx")),
        check_vma=False,
    )
```
